32 devices in a mesh: batch: 2 (over x), head: 2 (over core), expert: 8 (over z, y).
Axes of the slice: x: 2, y: 2, z: 4, core: 2. Of those that a mesh axis runs over, the one named last changes fastest.
Arguments:
- hidden_in: bfloat16 [4096, 2048], P(('batch', 'head', 'expert')), may hold values from -6 to 6
- norm_gain: float32 [2048], replicated, may hold values from 0.25 to 1.75
- w_gate: bfloat16 [16, 2048, 384], P('expert', ('batch', 'head')), may hold values from -0.125 to 0.125
- w_up: bfloat16 [16, 2048, 384], P('expert', ('batch', 'head')), may hold values from -0.125 to 0.125
- w_down: bfloat16 [16, 384, 2048], P('expert', None, ('batch', 'head')), may hold values from -0.3125 to 0.3125
- expert_ids: int32 [4096, 2], P(('batch', 'head', 'expert')), may hold values from 0 to 15, all different within a row; in each aligned block of 128 rows (0 to 127, 128 to 255, ...) at most 24 rows name the same one
- gate_codes: int32 [4096, 2], P(('batch', 'head', 'expert')), may hold values from 4096 to 65535
- out_grad: bfloat16 [4096, 2048], P(('batch', 'head', 'expert')), may hold values from -6 to 6
Outputs:
- output: bfloat16 [4096, 2048], P(('batch', 'head', 'expert'))
- grad_in: bfloat16 [4096, 2048], P(('batch', 'head', 'expert'))
The draws below stay inside these ranges and needn't reach their ends.
Inputs may be any that keep to these rules, and one draw needn't show every extreme that they name: `expert_ids`: each row names 2 different experts; within the rows of one device no expert is named more than 24 times, a bound that some block reaches.
All inputs are finite; a program needn't handle non-finite values.
Results may differ from the reference program's by a relative error of at most 0.0055.
Values may be sent and summed in bfloat16 or wider, within the bound.
A program may use at most 128 MiB of HBM per device.

```python
import math
import jax
import jax.numpy as jnp
import numpy as np
from jax import lax

D = 2048
FW = 384
TOP = 2
TOK_DEV = 128
EXPERTS = 16
CAP = 24
TOKENS = 4096


def touch_ends(values, key, low, high):
    place = [jax.random.randint(jax.random.fold_in(key, axis), (), 0, length) for axis, length in enumerate(values.shape)]
    main_axis = values.shape.index(max(values.shape))
    neighbour = place[:main_axis] + [(place[main_axis] + 1) % values.shape[main_axis]] + place[main_axis + 1:]
    return values.at[tuple(place)].set(low).at[tuple(neighbour)].set(high)


def level_of(stream_key, dims, split, least, top_value):
    gain = 1.0
    for dim, blocks in split:
        heights = jax.random.uniform(jax.random.fold_in(jax.random.fold_in(stream_key, 6), dim), (blocks,), jnp.float32, least / len(split), top_value / len(split))
        gain = gain * jnp.repeat(jnp.exp(heights), dims[dim] // blocks).reshape((-1,) + (1,) * (len(dims) - 1 - dim))
    return gain


def routed_block(stream_key, own, number, rows, count, top, most, slope):
    sequence = jax.random.permutation(stream_key, count)
    crowded, ordinary = portions_of(count, rows * top, most, slope, True), portions_of(count, rows * top, most, slope, False)
    places = jnp.arange(count)

    def named(sizes, rotation):
        used = int((sizes > 0).sum())
        fixed = max(1, used // 4)
        moved = fixed + (places - fixed + rotation * (used - fixed)) % max(1, count - fixed)
        return jnp.zeros((count,), jnp.int32).at[sequence[jnp.where(places < fixed, places, moved)]].set(jnp.asarray(sizes, jnp.int32))

    sizes = jnp.where(number % 4 == 0, named(crowded, number // 4), named(ordinary, number - number // 4 - 1))
    mixed = jax.random.permutation(jax.random.fold_in(own, 3), count)
    donor, sink = mixed[0:count // 2 * 2:2], mixed[1:count // 2 * 2:2]
    slack = jnp.minimum(sizes[donor] - 1, most - sizes[sink]) // 2
    slack = jnp.where((donor == sequence[0]) | (sink == sequence[0]) | (sizes[sink] == 0), 0, jnp.maximum(slack, 0))
    moved = jax.random.randint(jax.random.fold_in(own, 4), (count // 2,), 0, 1 << 20) % (slack + 1)
    sizes = sizes.at[donor].add(-moved).at[sink].add(moved)
    items = jnp.searchsorted(jnp.cumsum(sizes), jnp.arange(rows * top), side="right").astype(jnp.int32)
    table = items.reshape(top, rows).T
    table = table[jax.random.permutation(jax.random.fold_in(own, 1), rows)]
    rotation = jax.random.randint(jax.random.fold_in(own, 2), (rows, 1), 0, top)
    return jnp.take_along_axis(table, (jnp.arange(top)[None, :] + rotation) % top, axis=1)


def portions_of(amount, total, limit, slope, full):
    weights = [(1 << 20) // math.isqrt(rank ** slope) + 1 for rank in range(1, amount + 1)]
    largest = limit if full else min(limit, max(-(-total // amount), total * weights[0] // sum(weights)))
    least = 1 if total - largest >= amount - 1 else 0
    holding, rest = [largest] + [least] * (amount - 1), total - largest - least * (amount - 1)
    while rest > 0:
        movable = [i for i in range(1, amount) if holding[i] < largest] or [i for i in range(1, amount) if holding[i] < limit]
        pool, left = sum([weights[i] for i in movable]), rest
        for i in movable:
            more = min(limit - holding[i], max(1, left * weights[i] // pool), rest)
            holding[i] = holding[i] + more
            rest = rest - more
    return np.array(holding)


def noise(key, dims, spread, limit, shards=(), kind=jnp.bfloat16):
    array = spread * jax.random.normal(key, dims, jnp.float32)
    if shards:
        array = array * level_of(key, dims, shards, -0.22, 0.18)
    return jnp.clip(array, -limit, limit).astype(kind)


def setup_inputs(seed: int = 0) -> dict:
    splits = jax.random.split(jax.random.key(seed), 9)
    hidden_in = noise(splits[0], (TOKENS, D), 1.0, 6.0, ((0, 32),))
    norm_gain = jnp.clip(1.0 + 0.15 * jax.random.normal(splits[1], (D,), jnp.float32), 0.25, 1.75)
    w_gate = noise(splits[2], (EXPERTS, D, FW), D ** -0.5, 0.125, ((0, 8), (1, 4)))
    w_up = noise(splits[3], (EXPERTS, D, FW), D ** -0.5, 0.125, ((0, 8), (1, 4)))
    w_down = noise(splits[4], (EXPERTS, FW, D), FW ** -0.5, 0.3125, ((0, 8), (2, 4)))
    expert_ids_keys = jax.random.split(jax.random.fold_in(splits[5], 1), TOKENS // TOK_DEV)
    expert_ids_turns = jax.random.permutation(jax.random.fold_in(splits[5], 3), TOKENS // TOK_DEV)
    expert_ids = jax.vmap(lambda own, number: routed_block(jax.random.fold_in(splits[5], 2), own, number, TOK_DEV, EXPERTS, TOP, CAP, 2))(expert_ids_keys, expert_ids_turns).reshape((TOKENS, TOP))
    gate_codes = touch_ends(jax.random.randint(splits[6], (TOKENS, TOP), 4096, 65536), jax.random.fold_in(splits[6], 1), 4096, 65535).astype(jnp.int32)
    out_grad = noise(splits[7], (TOKENS, D), 1.0, 6.0, ((0, 32),))
    return dict(hidden_in=hidden_in, norm_gain=norm_gain, w_gate=w_gate, w_up=w_up, w_down=w_down, expert_ids=expert_ids, gate_codes=gate_codes, out_grad=out_grad)


epsilon = 1e-06

def slot_tables(expert_ids, expert_total, capacity):
    chosen = expert_ids.shape[1]
    routes = expert_ids.reshape(-1).astype(jnp.int32)
    route_total = routes.shape[0]
    labels = jnp.arange(expert_total, dtype=jnp.int32)
    onehot = (routes[:, None] == labels[None, :]).astype(jnp.int32)
    before = (jnp.cumsum(onehot, axis=0) - onehot).astype(jnp.int32)
    position = lax.optimization_barrier(jnp.sum(before * onehot, axis=1)).astype(jnp.int32)
    slot_ids = (routes * capacity + position).astype(jnp.int32)
    owner_rows = (jnp.arange(route_total, dtype=jnp.int32) // chosen).astype(jnp.int32)
    source_rows = jnp.zeros((expert_total * capacity,), jnp.int32).at[slot_ids].set(owner_rows)
    filled = jnp.zeros((expert_total * capacity,), jnp.int32).at[slot_ids].set(1)
    return (slot_ids, source_rows, filled)

def expert_forward(slot_rows, gate_mat, up_mat, down_mat):
    gate_pre = jnp.dot(slot_rows, gate_mat, preferred_element_type=jnp.float32)
    up_pre = jnp.dot(slot_rows, up_mat, preferred_element_type=jnp.float32)
    inner_rows = (jax.nn.silu(gate_pre) * up_pre).astype(jnp.bfloat16)
    result = jnp.dot(inner_rows, down_mat, preferred_element_type=jnp.float32).astype(jnp.bfloat16)
    return (result, gate_pre, up_pre)

def expert_backward(slot_grads, gate_pre, up_pre, gate_mat, up_mat, down_mat):
    back_grad = jnp.dot(slot_grads, down_mat.T, preferred_element_type=jnp.float32)
    sigmoid_gate = jax.nn.sigmoid(gate_pre)
    grad_gate = (back_grad * up_pre * sigmoid_gate * (1.0 + gate_pre * (1.0 - sigmoid_gate))).astype(jnp.bfloat16)
    grad_up = (back_grad * jax.nn.silu(gate_pre)).astype(jnp.bfloat16)
    grad_rows = jnp.dot(grad_gate, gate_mat.T, preferred_element_type=jnp.float32)
    grad_rows = grad_rows + jnp.dot(grad_up, up_mat.T, preferred_element_type=jnp.float32)
    return grad_rows.astype(jnp.bfloat16)

def place_weights(slot_block, weight_block):
    return jnp.zeros((EXPERTS * CAP,), jnp.float32).at[slot_block].set(weight_block)

def reference(hidden_in, norm_gain, w_gate, w_up, w_down, expert_ids, gate_codes, out_grad):
    blocks = TOKENS // TOK_DEV
    hidden_float = hidden_in.astype(jnp.float32)
    row_scale = lax.rsqrt(lax.optimization_barrier(jnp.mean(hidden_float * hidden_float, axis=1, keepdims=True)) + epsilon)
    gain_float = norm_gain.astype(jnp.float32)
    normed = (hidden_float * row_scale * gain_float).astype(jnp.bfloat16)
    code_values = gate_codes.astype(jnp.float32)
    weights = code_values / lax.optimization_barrier(jnp.sum(code_values, axis=1, keepdims=True))
    tables = jax.vmap(slot_tables, in_axes=(0, None, None))(expert_ids.reshape(blocks, TOK_DEV, TOP), EXPERTS, CAP)
    slot_ids, source_rows, filled = tables
    slot_weights = jax.vmap(place_weights)(slot_ids, weights.reshape(blocks, TOK_DEV * TOP))
    offsets = (jnp.arange(blocks, dtype=jnp.int32) * TOK_DEV)[:, None]
    token_rows = (source_rows + offsets).astype(jnp.int32)

    def one_expert(totals, members):
        gate_mat, up_mat, down_mat, expert_index = members
        start = (expert_index * CAP).astype(jnp.int32)
        rows_index = lax.dynamic_slice_in_dim(token_rows, start, CAP, 1).reshape(-1)
        live = lax.dynamic_slice_in_dim(filled, start, CAP, 1).reshape(-1)
        share = lax.dynamic_slice_in_dim(slot_weights, start, CAP, 1).reshape(-1)
        keep = (live == 1)[:, None]
        nothing = jnp.zeros((), jnp.bfloat16)
        slot_rows = jnp.where(keep, normed[rows_index], nothing)
        slot_grads = jnp.where(keep, out_grad[rows_index], nothing)
        result, gate_pre, up_pre = expert_forward(slot_rows, gate_mat, up_mat, down_mat)
        grad_rows = expert_backward(slot_grads, gate_pre, up_pre, gate_mat, up_mat, down_mat)
        mixture, grad_normed = totals
        mixture = mixture.at[rows_index].add(share[:, None] * result.astype(jnp.float32))
        grad_normed = grad_normed.at[rows_index].add(share[:, None] * grad_rows.astype(jnp.float32))
        return ((mixture, grad_normed), None)
    start_totals = (jnp.zeros((TOKENS, D), jnp.float32), jnp.zeros((TOKENS, D), jnp.float32))
    members = (w_gate, w_up, w_down, jnp.arange(EXPERTS, dtype=jnp.int32))
    final_totals = lax.scan(one_expert, start_totals, members)[0]
    mixture, grad_normed = final_totals
    output = (hidden_float + mixture).astype(jnp.bfloat16)
    scaled = gain_float * grad_normed
    inner_mean = lax.optimization_barrier(jnp.mean(scaled * hidden_float, axis=1, keepdims=True))
    grad_in = out_grad.astype(jnp.float32) + row_scale * scaled - hidden_float * (row_scale * row_scale * row_scale) * inner_mean
    return (output, grad_in.astype(jnp.bfloat16))
```

```python
import functools

import jax
import jax.numpy as jnp
import numpy as np
from jax import lax
from jax.experimental import pallas as pl
from jax.experimental.pallas import tpu as pltpu
from jax.sharding import PartitionSpec as P

epsilon = 1e-06
MESH = pl.DeviceIdType.MESH
BF = jnp.bfloat16
F32 = jnp.float32
NN = (((1,), (0,)), ((), ()))
NT = (((1,), (1,)), ((), ()))
TN = (((0,), (0,)), ((), ()))


def mm(a, b, dims=NN):
    return lax.dot_general(a, b, dims, preferred_element_type=F32)


def kernel(
    sizes, hid, gain, wg_in, wu_in, wd_in, ids, codes, og, base, pick, place, out, gin,
    wg, wu, wd, send_n, send_g, recv_n, recv_g, res, gres, ret, gret, gp, up, scaled, table,
    s_sem, r_sem, own_sem, wb_send, wh_send, w_recv, w_own,
):
    n, nb, nh, cap, rows, local = sizes
    me, mb, mh = (lax.axis_index(a) for a in ("expert", "batch", "head"))
    tok, features = hid.shape
    chunks = nb * nh
    width = features // chunks
    mine = mb * nh + mh
    peers = (("expert", me, n), ("batch", mb, nb), ("head", mh, nh))

    barrier = pltpu.get_barrier_semaphore()
    for axis, at, count in peers:
        @pl.loop(1, count)
        def _(k, axis=axis, at=at, count=count):
            pl.semaphore_signal(
                barrier, inc=1, device_id={axis: lax.rem(at + k, count)}, device_id_type=MESH
            )
    pl.semaphore_wait(barrier, n + nb + nh - 3)

    tensors = ((wg_in, wg), (wu_in, wu), (wd_in, wd))

    def to_batch(i, k):
        src, dst = tensors[i]
        other = lax.rem(mb + k, nb)
        return pltpu.make_async_remote_copy(
            src_ref=src, dst_ref=dst.at[mine], send_sem=wb_send.at[i, k], recv_sem=w_recv.at[i, mine],
            device_id={"batch": other}, device_id_type=MESH,
        )

    def to_head(i, j, k):
        src, dst = tensors[i]
        b = lax.rem(mb + j, nb)
        slot = b * nh + mh
        return pltpu.make_async_remote_copy(
            src_ref=src if j == 0 else dst.at[slot], dst_ref=dst.at[slot],
            send_sem=wh_send.at[i, j, k], recv_sem=w_recv.at[i, slot],
            device_id={"head": lax.rem(mh + k, nh)}, device_id_type=MESH,
        )

    def arrived(i, slot):
        dst = tensors[i][1].at[slot]
        pltpu.make_async_copy(dst, dst, w_recv.at[i, slot]).wait()

    def keep_own(i):
        return pltpu.make_async_copy(tensors[i][0], tensors[i][1].at[mine], w_own.at[i])

    for i in range(3):
        @pl.loop(1, nb)
        def _(k, i=i):
            to_batch(i, k).start()
        keep_own(i).start()

    def block(ref, d):
        return ref.at[pl.ds(pl.multiple_of(d * rows, 16), rows)]

    def row_copy(step, src, dst, k):
        other = lax.rem(me + k, n)
        return pltpu.make_async_remote_copy(
            src_ref=block(src, other), dst_ref=block(dst, me),
            send_sem=s_sem.at[step, k], recv_sem=r_sem.at[step, k],
            device_id={"expert": other}, device_id_type=MESH,
        )

    flows = ((send_n, recv_n), (send_g, recv_g), (res, ret), (gres, gret))

    def own_copy(step):
        src, dst = flows[step]
        return pltpu.make_async_copy(block(src, me), block(dst, me), own_sem.at[step])

    def start(step):
        @pl.loop(1, n)
        def _(k):
            row_copy(step, *flows[step], k).start()
        own_copy(step).start()

    def finish(step):
        @pl.loop(1, n)
        def _(k):
            dst = block(flows[step][1], lax.rem(me + n - k, n))
            pltpu.make_async_copy(dst, dst, r_sem.at[step, k]).wait()
        own_copy(step).wait()

    def cols(c):
        return pl.ds(pl.multiple_of(c * width, 128), width)

    experts = base.shape[1]
    chosen = ids.shape[1]
    lanes = lax.broadcasted_iota(jnp.int32, (tok, experts), 1)
    hits = [(ids[:, k:k + 1] == lanes).astype(F32) for k in range(chosen)]
    total = functools.reduce(jnp.add, hits)
    earlier = (
        lax.broadcasted_iota(jnp.int32, (tok, tok), 1) < lax.broadcasted_iota(jnp.int32, (tok, tok), 0)
    ).astype(F32).astype(BF)
    where = mm(earlier, total.astype(BF)) + base[...]
    slots = lax.broadcasted_iota(jnp.int32, (tok, n * rows), 1).astype(F32)
    marks = [(slots == jnp.sum(where * h, axis=1, keepdims=True)).astype(F32) for h in hits]
    table[...] = functools.reduce(jnp.add, marks).astype(BF)

    def square(c, acc):
        v = hid[:, cols(c)].astype(F32)
        return acc + jnp.sum(v * v, axis=1, keepdims=True)

    zero = jnp.zeros((tok, 1), F32)
    scale = lax.rsqrt(lax.fori_loop(0, chunks, square, zero) / features + epsilon)

    @pl.loop(0, chunks)
    def _(c):
        v = (hid[:, cols(c)].astype(F32) * scale * gain[:, cols(c)]).astype(BF)
        send_n[:, cols(c)] = mm(table[...], v, TN).astype(BF)
    start(0)

    @pl.loop(0, chunks)
    def _(c):
        send_g[:, cols(c)] = mm(table[...], og[:, cols(c)], TN).astype(BF)
    start(1)

    for i in range(3):
        for j in range(nb):
            if j > 0:
                arrived(i, lax.rem(mb + j, nb) * nh + mh)
            for k in range(1, nh):
                to_head(i, j, k).start()
    for i in range(3):
        keep_own(i).wait()
        for b in range(nb):
            for k in range(1, nh):
                arrived(i, b * nh + lax.rem(mh + k, nh))

    finish(0)
    gp[...] = jnp.zeros_like(gp)
    up[...] = jnp.zeros_like(up)

    @pl.loop(0, chunks)
    def _(c):
        x = recv_n[:, cols(c)]
        for e in range(local):
            xe = mm(pick[e], x).astype(BF)
            gp[e] += mm(xe, wg[c, e])
            up[e] += mm(xe, wu[c, e])

    inner = [(jax.nn.silu(gp[e]) * up[e]).astype(BF) for e in range(local)]

    @pl.loop(0, chunks)
    def _(c):
        parts = [mm(place[e], mm(inner[e], wd[c, e]).astype(BF)) for e in range(local)]
        res[:, cols(c)] = functools.reduce(jnp.add, parts).astype(BF)
    start(2)

    finish(1)

    def back(c, acc):
        y = recv_g[:, cols(c)]
        return tuple(
            acc[e] + mm(mm(pick[e], y).astype(BF), wd[c, e], NT) for e in range(local)
        )

    none = tuple(jnp.zeros(gp.shape[1:], F32) for _ in range(local))
    grads = lax.fori_loop(0, chunks, back, none)
    g_gate, g_up = [], []
    for e in range(local):
        g = gp[e]
        s = jax.nn.sigmoid(g)
        g_gate.append((grads[e] * up[e] * s * (1.0 + g * (1.0 - s))).astype(BF))
        g_up.append((grads[e] * (g * s)).astype(BF))

    @pl.loop(0, chunks)
    def _(c):
        parts = []
        for e in range(local):
            r = mm(g_gate[e], wg[c, e], NT) + mm(g_up[e], wu[c, e], NT)
            parts.append(mm(place[e], r.astype(BF)))
        gres[:, cols(c)] = functools.reduce(jnp.add, parts).astype(BF)
    start(3)

    code = codes[...].astype(F32)
    share = code / jnp.sum(code, axis=1, keepdims=True)
    mix = functools.reduce(jnp.add, [m * share[:, k:k + 1] for k, m in enumerate(marks)])
    high = mix.astype(BF)
    low = (mix - high.astype(F32)).astype(BF)

    finish(2)

    @pl.loop(0, chunks)
    def _(c):
        x = ret[:, cols(c)]
        out[:, cols(c)] = (hid[:, cols(c)].astype(F32) + mm(high, x) + mm(low, x)).astype(BF)

    finish(3)

    def scaling(c, acc):
        x = gret[:, cols(c)]
        a = gain[:, cols(c)] * (mm(high, x) + mm(low, x))
        scaled[:, cols(c)] = a
        return acc + jnp.sum(a * hid[:, cols(c)].astype(F32), axis=1, keepdims=True)

    mean = lax.fori_loop(0, chunks, scaling, zero) / features
    cubed = scale * scale * scale * mean

    @pl.loop(0, chunks)
    def _(c):
        gin[:, cols(c)] = (
            og[:, cols(c)].astype(F32) + scale * scaled[:, cols(c)] - hid[:, cols(c)].astype(F32) * cubed
        ).astype(BF)

    for step in range(4):
        @pl.loop(1, n)
        def _(k, step=step):
            row_copy(step, *flows[step], k).wait_send()
    for i in range(3):
        @pl.loop(1, nb)
        def _(k, i=i):
            to_batch(i, k).wait_send()
        for j in range(nb):
            for k in range(1, nh):
                to_head(i, j, k).wait_send()


def body(hidden_in, norm_gain, w_gate, w_up, w_down, expert_ids, gate_codes, out_grad):
    n, nb, nh = (lax.axis_size(a) for a in ("expert", "batch", "head"))
    local, width, hidden = w_gate.shape
    experts = n * local
    tok, features = hidden_in.shape
    chosen = expert_ids.shape[1]
    cap = 3 * tok * chosen // (2 * experts)
    rows = -(-local * cap // 16) * 16
    chunks = nb * nh
    numbers = np.arange(experts)
    base = (numbers // local * rows + numbers % local * cap).astype(np.float32)[None]
    pick = np.zeros((local, n * cap, n * rows), np.float32)
    for e in range(local):
        line = np.arange(n * cap)
        pick[e, line, line // cap * rows + e * cap + line % cap] = 1.0
    place = pick.transpose(0, 2, 1)
    flow = pltpu.VMEM((n * rows, features), BF)
    vmem = pl.BlockSpec(memory_space=pltpu.VMEM)
    hbm = pl.BlockSpec(memory_space=pl.ANY)
    dma = pltpu.SemaphoreType.DMA
    out_type = jax.ShapeDtypeStruct((tok, features), BF)
    return pl.pallas_call(
        functools.partial(kernel, (n, nb, nh, cap, rows, local)),
        out_shape=(out_type, out_type),
        in_specs=[vmem, vmem, hbm, hbm, hbm] + [vmem] * 6,
        out_specs=(vmem, vmem),
        scratch_shapes=[
            pltpu.VMEM((chunks, local, width, hidden), BF),
            pltpu.VMEM((chunks, local, width, hidden), BF),
            pltpu.VMEM((chunks, local, hidden, width), BF),
        ] + [flow] * 8 + [
            pltpu.VMEM((local, n * cap, hidden), F32),
            pltpu.VMEM((local, n * cap, hidden), F32),
            pltpu.VMEM((tok, features), F32),
            pltpu.VMEM((tok, n * rows), BF),
            dma((4, n)), dma((4, n)), dma((4,)),
            dma((3, nb)), dma((3, nb, nh)), dma((3, chunks)), dma((3,)),
        ],
        compiler_params=pltpu.CompilerParams(
            collective_id=0, has_side_effects=True, vmem_limit_bytes=60 * 1024 * 1024
        ),
    )(
        hidden_in, norm_gain[None], w_gate, w_up, w_down, expert_ids, gate_codes, out_grad,
        jnp.asarray(base), jnp.asarray(pick, BF), jnp.asarray(place, BF),
    )


def solution(mesh):
    tokens = P(("batch", "head", "expert"), None)
    in_specs = (
        tokens,
        P(),
        P("expert", ("batch", "head"), None),
        P("expert", ("batch", "head"), None),
        P("expert", None, ("batch", "head")),
        tokens,
        tokens,
        tokens,
    )
    return jax.shard_map(body, mesh=mesh, in_specs=in_specs, out_specs=(tokens, tokens), check_vma=False)
```

```python
import functools

import jax
import jax.numpy as jnp
import numpy as np
from jax import lax
from jax.experimental import pallas as pl
from jax.experimental.pallas import tpu as pltpu
from jax.sharding import PartitionSpec as P

epsilon = 1e-06
MESH = pl.DeviceIdType.MESH
BF = jnp.bfloat16
F32 = jnp.float32
NN = (((1,), (0,)), ((), ()))
NT = (((1,), (1,)), ((), ()))
TN = (((0,), (0,)), ((), ()))


def mm(a, b, dims=NN):
    return lax.dot_general(a, b, dims, preferred_element_type=F32)


def kernel(
    sizes, hid, gain, wg_in, wu_in, wd_in, meta, og, base, pick, place, out, gin,
    wg, wu, wd, send_n, recv_n, recv_g, res, gres, gret, send_g, ret, pass_g, pass_r,
    far_og, far_part, far_sum, far_meta, gp, up, scaled, table,
    s_sem, r_sem, pass_send, part_recv, og_sem, sum_sem, meta_sem, wb_send, wh_send, w_recv, w_own,
):
    n, nb, nh, cap, rows, local, chosen = sizes
    me, mb, mh = (lax.axis_index(a) for a in ("expert", "batch", "head"))
    tok, features = hid.shape
    chunks = nb * nh
    width = features // chunks
    mine = mb * nh + mh
    peers = (("expert", me, n), ("batch", mb, nb), ("head", mh, nh))

    barrier = pltpu.get_barrier_semaphore()
    for axis, at, count in peers:
        @pl.loop(1, count)
        def _(k, axis=axis, at=at, count=count):
            pl.semaphore_signal(
                barrier, inc=1, device_id={axis: lax.rem(at + k, count)}, device_id_type=MESH
            )
    pl.semaphore_wait(barrier, n + nb + nh - 3)

    tensors = ((wg_in, wg), (wu_in, wu), (wd_in, wd))

    def to_batch(i, k):
        src, dst = tensors[i]
        other = lax.rem(mb + k, nb)
        return pltpu.make_async_remote_copy(
            src_ref=src, dst_ref=dst.at[mine], send_sem=wb_send.at[i, k], recv_sem=w_recv.at[i, mine],
            device_id={"batch": other}, device_id_type=MESH,
        )

    def to_head(i, j, k):
        src, dst = tensors[i]
        b = lax.rem(mb + j, nb)
        slot = b * nh + mh
        return pltpu.make_async_remote_copy(
            src_ref=src if j == 0 else dst.at[slot], dst_ref=dst.at[slot],
            send_sem=wh_send.at[i, j, k], recv_sem=w_recv.at[i, slot],
            device_id={"head": lax.rem(mh + k, nh)}, device_id_type=MESH,
        )

    def arrived(i, slot):
        dst = tensors[i][1].at[slot]
        pltpu.make_async_copy(dst, dst, w_recv.at[i, slot]).wait()

    def keep_own(i):
        return pltpu.make_async_copy(tensors[i][0], tensors[i][1].at[mine], w_own.at[i])

    quarter, half = n // 4, n // 2
    side, lane, q = me // half, lax.rem(me, quarter), me // quarter
    first = side * half
    relays = q == 1 + side
    turn = (1 - side) * (1 - q) + side * (q - 2)
    beyond = (2 - side) * quarter + lane

    def source(d):
        return ((2 - side) + d * (1 - 2 * side)) * quarter + lane

    def remote(src, dst, send, recv, other):
        return pltpu.make_async_remote_copy(
            src_ref=src, dst_ref=dst, send_sem=send, recv_sem=recv,
            device_id={"expert": other}, device_id_type=MESH,
        )

    def meta_out():
        return remote(meta, far_meta.at[turn], meta_sem.at[0], meta_sem.at[1 + turn], beyond)

    def og_out():
        return remote(og, far_og.at[turn], og_sem.at[0], og_sem.at[1 + turn], beyond)

    def wait(ref, sem):
        pltpu.make_async_copy(ref, ref, sem).wait()

    meta_out().start()
    og_out().start()
    for i in range(3):
        @pl.loop(1, nb)
        def _(k, i=i):
            to_batch(i, k).start()
        keep_own(i).start()

    def block(ref, d):
        return ref.at[pl.ds(pl.multiple_of(d * rows, 16), rows)]

    def near(k):
        return first + lax.rem(me - first + k, half)

    def direct(step, k):
        if step == 0 or step == 3:
            src, dst = ((send_n, recv_n), None, None, (gres, gret))[step]
            other = lax.rem(me + k, n)
            src, dst = block(src, other), block(dst, me)
        elif step == 1:
            other = near(k)
            src, dst = block(send_g, other - first), block(recv_g, me)
        else:
            other = near(k)
            src, dst = block(res, other), block(ret, me - first)
        return remote(src, dst, s_sem.at[step, other], r_sem.at[step, me], other)

    homes = ((send_n, recv_n), (send_g, recv_g), (res, ret), (gres, gret))
    spans = (n, half, half, n)

    def start(step):
        @pl.loop(1, spans[step])
        def _(k):
            direct(step, k).start()
        src, dst = homes[step]
        at = (me, me - first, me, me)[step], (me, me, me - first, me)[step]
        pltpu.make_async_copy(block(src, at[0]), block(dst, at[1]), r_sem.at[step, me]).start()

    def finish(step):
        dst = homes[step][1]
        @pl.loop(0, half if step == 2 else n)
        def _(j):
            wait(block(dst, j), r_sem.at[step, j + first if step == 2 else j])

    def pass_on(d, k):
        other = near(k)
        return remote(
            block(pass_g.at[d], other - first), block(recv_g, source(d)),
            pass_send.at[0, d, k], r_sem.at[1, source(d)], other,
        )

    def to_relay(k):
        s = half - first + k
        qs = s // quarter
        d = side * (1 - qs) + (1 - side) * (qs - 2)
        other = (1 + side) * quarter + lax.rem(s, quarter)
        src, dst = block(res, s), block(pass_r.at[d], me - first)
        recv = part_recv.at[d, me - first]
        return other, src, dst, s_sem.at[2, s], recv

    def sum_out(d):
        return remote(far_sum.at[d], far_part, pass_send.at[1, d, 0], sum_sem.at[0], source(d))

    def cols(c):
        return pl.ds(pl.multiple_of(c * width, 128), width)

    experts = base.shape[0]
    lower = (
        lax.broadcasted_iota(jnp.int32, (tok, tok), 0) < lax.broadcasted_iota(jnp.int32, (tok, tok), 1)
    ).astype(F32).astype(BF)

    def routing(words, begin, count):
        labels = lax.broadcasted_iota(jnp.int32, (experts, tok), 0)
        hits = [(words[k:k + 1] == labels).astype(F32) for k in range(chosen)]
        where = mm(functools.reduce(jnp.add, hits).astype(BF), lower) + base[...]
        slots = (lax.broadcasted_iota(jnp.int32, (count, tok), 0) + begin).astype(F32)
        marks = [(slots == jnp.sum(where * h, axis=0, keepdims=True)).astype(F32) for h in hits]
        code = [words[chosen + k:chosen + k + 1].astype(F32) for k in range(chosen)]
        total = functools.reduce(jnp.add, code)
        mix = functools.reduce(jnp.add, [m * (w / total) for m, w in zip(marks, code)])
        high = mix.astype(BF)
        low = (mix - high.astype(F32)).astype(BF)
        return functools.reduce(jnp.add, marks).astype(BF), high, low

    def combine(high, low, x):
        return mm(high, x, TN) + mm(low, x, TN)

    table[0], table[1], table[2] = routing(meta[...], 0, n * rows)
    own = pl.ds(pl.multiple_of(first * rows, 16), half * rows)

    def square(c, acc):
        v = hid[:, cols(c)].astype(F32)
        return acc + jnp.sum(v * v, axis=1, keepdims=True)

    zero = jnp.zeros((tok, 1), F32)
    scale = lax.rsqrt(lax.fori_loop(0, chunks, square, zero) / features + epsilon)

    @pl.loop(0, chunks)
    def _(c):
        v = (hid[:, cols(c)].astype(F32) * scale * gain[:, cols(c)]).astype(BF)
        send_n[:, cols(c)] = mm(table[0], v).astype(BF)
    start(0)

    @pl.loop(0, chunks)
    def _(c):
        send_g[:, cols(c)] = mm(table[0, own], og[:, cols(c)]).astype(BF)
    start(1)

    def forward_on(i):
        for j in range(nb):
            if j > 0:
                arrived(i, lax.rem(mb + j, nb) * nh + mh)
            for k in range(1, nh):
                to_head(i, j, k).start()

    def whole(i):
        keep_own(i).wait()
        for b in range(nb):
            for k in range(1, nh):
                arrived(i, b * nh + lax.rem(mh + k, nh))

    forward_on(0)

    @pl.when(relays)
    def _():
        for d in range(2):
            wait(far_meta.at[d], meta_sem.at[1 + d])
            wait(far_og.at[d], og_sem.at[1 + d])
            spread = routing(far_meta[d], first * rows, half * rows)[0]

            @pl.loop(0, chunks)
            def _(c, d=d, spread=spread):
                pass_g[d, :, cols(c)] = mm(spread, far_og[d, :, cols(c)]).astype(BF)

            @pl.loop(1, half)
            def _(k, d=d):
                pass_on(d, k).start()
            pltpu.make_async_copy(
                block(pass_g.at[d], me - first), block(recv_g, source(d)), r_sem.at[1, source(d)]
            ).start()

    forward_on(1)
    forward_on(2)
    finish(0)
    whole(0)
    whole(1)
    gp[...] = jnp.zeros_like(gp)
    up[...] = jnp.zeros_like(up)

    @pl.loop(0, chunks)
    def _(c):
        x = recv_n[:, cols(c)]
        for e in range(local):
            xe = mm(pick[e], x).astype(BF)
            gp[e] += mm(xe, wg[c, e])
            up[e] += mm(xe, wu[c, e])

    whole(2)
    inner = [(jax.nn.silu(gp[e]) * up[e]).astype(BF) for e in range(local)]

    @pl.loop(0, chunks)
    def _(c):
        parts = [mm(place[e], mm(inner[e], wd[c, e]).astype(BF)) for e in range(local)]
        res[:, cols(c)] = functools.reduce(jnp.add, parts).astype(BF)

    @pl.loop(0, half)
    def _(k):
        other, src, dst, send, recv = to_relay(k)

        @pl.when(other != me)
        def _():
            remote(src, dst, send, recv, other).start()

        @pl.when(other == me)
        def _():
            pltpu.make_async_copy(src, dst, recv).start()
    start(2)

    finish(1)

    def back(c, acc):
        y = recv_g[:, cols(c)]
        return tuple(
            acc[e] + mm(mm(pick[e], y).astype(BF), wd[c, e], NT) for e in range(local)
        )

    none = tuple(jnp.zeros(gp.shape[1:], F32) for _ in range(local))
    grads = lax.fori_loop(0, chunks, back, none)
    g_gate, g_up = [], []
    for e in range(local):
        g = gp[e]
        s = jax.nn.sigmoid(g)
        g_gate.append((grads[e] * up[e] * s * (1.0 + g * (1.0 - s))).astype(BF))
        g_up.append((grads[e] * (g * s)).astype(BF))

    @pl.loop(0, chunks)
    def _(c):
        parts = []
        for e in range(local):
            r = mm(g_gate[e], wg[c, e], NT) + mm(g_up[e], wu[c, e], NT)
            parts.append(mm(place[e], r.astype(BF)))
        gres[:, cols(c)] = functools.reduce(jnp.add, parts).astype(BF)
    start(3)

    @pl.when(relays)
    def _():
        for d in range(2):
            @pl.loop(0, half)
            def _(j, d=d):
                wait(block(pass_r.at[d], j), part_recv.at[d, j])
            _, high, low = routing(far_meta[d], first * rows, half * rows)

            @pl.loop(0, chunks)
            def _(c, d=d, high=high, low=low):
                far_sum[d, :, cols(c)] = combine(high, low, pass_r[d, :, cols(c)]).astype(BF)
            sum_out(d).start()

    finish(2)
    wait(far_part, sum_sem.at[0])

    @pl.loop(0, chunks)
    def _(c):
        mixture = combine(table[1, own], table[2, own], ret[:, cols(c)]) + far_part[:, cols(c)].astype(F32)
        out[:, cols(c)] = (hid[:, cols(c)].astype(F32) + mixture).astype(BF)

    finish(3)

    def scaling(c, acc):
        x = gret[:, cols(c)]
        a = gain[:, cols(c)] * combine(table[1], table[2], x)
        scaled[:, cols(c)] = a
        return acc + jnp.sum(a * hid[:, cols(c)].astype(F32), axis=1, keepdims=True)

    mean = lax.fori_loop(0, chunks, scaling, zero) / features
    cubed = scale * scale * scale * mean

    @pl.loop(0, chunks)
    def _(c):
        gin[:, cols(c)] = (
            og[:, cols(c)].astype(F32) + scale * scaled[:, cols(c)] - hid[:, cols(c)].astype(F32) * cubed
        ).astype(BF)

    for step in range(4):
        @pl.loop(1, spans[step])
        def _(k, step=step):
            direct(step, k).wait_send()

    @pl.loop(0, half)
    def _(k):
        other, src, dst, send, recv = to_relay(k)

        @pl.when(other != me)
        def _():
            remote(src, dst, send, recv, other).wait_send()
    meta_out().wait_send()
    og_out().wait_send()

    @pl.when(relays)
    def _():
        for d in range(2):
            @pl.loop(1, half)
            def _(k, d=d):
                pass_on(d, k).wait_send()
            sum_out(d).wait_send()

    for i in range(3):
        @pl.loop(1, nb)
        def _(k, i=i):
            to_batch(i, k).wait_send()
        for j in range(nb):
            for k in range(1, nh):
                to_head(i, j, k).wait_send()


def body(hidden_in, norm_gain, w_gate, w_up, w_down, expert_ids, gate_codes, out_grad):
    n, nb, nh = (lax.axis_size(a) for a in ("expert", "batch", "head"))
    local, width, hidden = w_gate.shape
    experts = n * local
    tok, features = hidden_in.shape
    chosen = expert_ids.shape[1]
    cap = 3 * tok * chosen // (2 * experts)
    rows = -(-local * cap // 16) * 16
    chunks = nb * nh
    meta = jnp.concatenate([expert_ids, gate_codes], axis=1).T
    meta = jnp.pad(meta, ((0, -2 * chosen % 8), (0, 0)))
    numbers = np.arange(experts)
    base = (numbers // local * rows + numbers % local * cap).astype(np.float32)[:, None]
    pick = np.zeros((local, n * cap, n * rows), np.float32)
    for e in range(local):
        line = np.arange(n * cap)
        pick[e, line, line // cap * rows + e * cap + line % cap] = 1.0
    place = pick.transpose(0, 2, 1)
    flow = pltpu.VMEM((n * rows, features), BF)
    vmem = pl.BlockSpec(memory_space=pltpu.VMEM)
    hbm = pl.BlockSpec(memory_space=pl.ANY)
    dma = pltpu.SemaphoreType.DMA
    out_type = jax.ShapeDtypeStruct((tok, features), BF)
    return pl.pallas_call(
        functools.partial(kernel, (n, nb, nh, cap, rows, local, chosen)),
        out_shape=(out_type, out_type),
        in_specs=[vmem, vmem, hbm, hbm, hbm] + [vmem] * 5,
        out_specs=(vmem, vmem),
        scratch_shapes=[
            pltpu.VMEM((chunks, local, width, hidden), BF),
            pltpu.VMEM((chunks, local, width, hidden), BF),
            pltpu.VMEM((chunks, local, hidden, width), BF),
        ] + [flow] * 6 + [
            pltpu.VMEM((n // 2 * rows, features), BF),
            pltpu.VMEM((n // 2 * rows, features), BF),
            pltpu.VMEM((2, n // 2 * rows, features), BF),
            pltpu.VMEM((2, n // 2 * rows, features), BF),
            pltpu.VMEM((2, tok, features), BF),
            pltpu.VMEM((tok, features), BF),
            pltpu.VMEM((2, tok, features), BF),
            pltpu.VMEM((2,) + meta.shape, jnp.int32),
            pltpu.VMEM((local, n * cap, hidden), F32),
            pltpu.VMEM((local, n * cap, hidden), F32),
            pltpu.VMEM((tok, features), F32),
            pltpu.VMEM((3, n * rows, tok), BF),
            dma((4, n)), dma((4, n)), dma((2, 2, n // 2)), dma((2, n // 2)),
            dma((3,)), dma((1,)), dma((3,)),
            dma((3, nb)), dma((3, nb, nh)), dma((3, chunks)), dma((3,)),
        ],
        compiler_params=pltpu.CompilerParams(
            collective_id=0, has_side_effects=True, vmem_limit_bytes=60 * 1024 * 1024
        ),
    )(
        hidden_in, norm_gain[None], w_gate, w_up, w_down, meta, out_grad,
        jnp.asarray(base), jnp.asarray(pick, BF), jnp.asarray(place, BF),
    )


def solution(mesh):
    tokens = P(("batch", "head", "expert"), None)
    in_specs = (
        tokens,
        P(),
        P("expert", ("batch", "head"), None),
        P("expert", ("batch", "head"), None),
        P("expert", None, ("batch", "head")),
        tokens,
        tokens,
        tokens,
    )
    return jax.shard_map(body, mesh=mesh, in_specs=in_specs, out_specs=(tokens, tokens), check_vma=False)
```

```python
import functools

import jax
import jax.numpy as jnp
import numpy as np
from jax import lax
from jax.experimental import pallas as pl
from jax.experimental.pallas import tpu as pltpu
from jax.sharding import PartitionSpec as P

epsilon = 1e-06
MESH = pl.DeviceIdType.MESH
BF = jnp.bfloat16
F32 = jnp.float32
NN = (((1,), (0,)), ((), ()))
NT = (((1,), (1,)), ((), ()))
TN = (((0,), (0,)), ((), ()))


def mm(a, b, dims=NN):
    return lax.dot_general(a, b, dims, preferred_element_type=F32)


def kernel(
    sizes, hid, gain, wg_in, wu_in, wd_in, meta, og, base, pick, place, out, gin,
    wg, wu, wd, send_n, recv_n, recv_g, res, gres, ret, send_g, gret, pass_g, pass_r,
    far_og, far_part, far_sum, far_meta, far_table, gp, up, scaled, table,
    s_sem, r_sem, near_sem, pass_send, part_send, part_recv, og_sem, sum_send, sum_recv, meta_sem, wb_send, wh_send, w_recv, w_own,
):
    n, nb, nh, cap, rows, local, chosen = sizes
    me, mb, mh = (lax.axis_index(a) for a in ("expert", "batch", "head"))
    tok, features = hid.shape
    chunks = nb * nh
    width = features // chunks
    mine = mb * nh + mh
    peers = (("expert", me, n), ("batch", mb, nb), ("head", mh, nh))

    barrier = pltpu.get_barrier_semaphore()
    for axis, at, count in peers:
        @pl.loop(1, count)
        def _(k, axis=axis, at=at, count=count):
            pl.semaphore_signal(
                barrier, inc=1, device_id={axis: lax.rem(at + k, count)}, device_id_type=MESH
            )
    pl.semaphore_wait(barrier, n + nb + nh - 3)

    tensors = ((wg_in, wg), (wu_in, wu), (wd_in, wd))

    def to_batch(i, k):
        src, dst = tensors[i]
        other = lax.rem(mb + k, nb)
        return pltpu.make_async_remote_copy(
            src_ref=src, dst_ref=dst.at[mine], send_sem=wb_send.at[i, k], recv_sem=w_recv.at[i, mine],
            device_id={"batch": other}, device_id_type=MESH,
        )

    def to_head(i, j, k):
        src, dst = tensors[i]
        b = lax.rem(mb + j, nb)
        slot = b * nh + mh
        return pltpu.make_async_remote_copy(
            src_ref=src if j == 0 else dst.at[slot], dst_ref=dst.at[slot],
            send_sem=wh_send.at[i, j, k], recv_sem=w_recv.at[i, slot],
            device_id={"head": lax.rem(mh + k, nh)}, device_id_type=MESH,
        )

    def arrived(i, slot):
        dst = tensors[i][1].at[slot]
        pltpu.make_async_copy(dst, dst, w_recv.at[i, slot]).wait()

    def keep_own(i):
        return pltpu.make_async_copy(tensors[i][0], tensors[i][1].at[mine], w_own.at[i])

    quarter, half = n // 4, n // 2
    side, lane, q = me // half, lax.rem(me, quarter), me // quarter
    first = side * half
    relays = q == 1 + side
    turn = (1 - side) * (1 - q) + side * (q - 2)
    beyond = (2 - side) * quarter + lane

    def cols(c):
        return pl.ds(pl.multiple_of(c * width, 128), width)

    def source(d):
        return ((2 - side) + d * (1 - 2 * side)) * quarter + lane

    def remote(src, dst, send, recv, other):
        return pltpu.make_async_remote_copy(
            src_ref=src, dst_ref=dst, send_sem=send, recv_sem=recv,
            device_id={"expert": other}, device_id_type=MESH,
        )

    def meta_out():
        return remote(meta, far_meta.at[turn], meta_sem.at[0], meta_sem.at[1 + turn], beyond)

    def og_out(c):
        return remote(
            og.at[:, cols(c)], far_og.at[turn, :, cols(c)], og_sem.at[0, c], og_sem.at[1 + turn, c], beyond
        )

    def wait(ref, sem):
        pltpu.make_async_copy(ref, ref, sem).wait()

    meta_out().start()
    for i in range(3):
        @pl.loop(1, nb)
        def _(k, i=i):
            to_batch(i, k).start()
        keep_own(i).start()

    def block(ref, d):
        return ref.at[pl.ds(pl.multiple_of(d * rows, 16), rows)]

    def near(k):
        return first + lax.rem(me - first + k, half)

    def direct(step, k):
        other = near(k)
        if step == 1:
            src, dst = block(send_g, other - first), block(recv_g, me)
        else:
            other = lax.rem(me + 1 + lax.rem(k + half - 2, n - 1), n)
            src, dst = ((send_n, recv_n), None, (res, ret))[step]
            src, dst = block(src, other), block(dst, me)
        return remote(src, dst, s_sem.at[step, other], r_sem.at[step, me], other)

    homes = ((send_n, recv_n), (send_g, recv_g), (res, ret))
    spans = (n, half, n)

    def start(step):
        @pl.loop(1, spans[step])
        def _(k):
            direct(step, k).start()
        src, dst = homes[step]
        at = me - first if step == 1 else me
        pltpu.make_async_copy(block(src, at), block(dst, me), r_sem.at[step, me]).start()

    def finish(step):
        dst = homes[step][1]

        @pl.loop(0, n)
        def _(j):
            wait(block(dst, j), r_sem.at[step, j])

    def piece(ref, j, c):
        return ref.at[pl.ds(pl.multiple_of(j * rows, 16), rows), cols(c)]

    def near_out(k, c):
        other = near(k)
        return remote(
            piece(gres, other, c), piece(gret, me - first, c),
            near_sem.at[0, k, c], near_sem.at[1, me - first, c], other,
        )

    def pass_on(d, k, c):
        other = near(k)
        return remote(
            piece(pass_g.at[d], other - first, c), piece(recv_g, source(d), c),
            pass_send.at[d, k, c], r_sem.at[1, source(d)], other,
        )

    def to_relay(k, c):
        s = half - first + k
        qs = s // quarter
        d = side * (1 - qs) + (1 - side) * (qs - 2)
        other = (1 + side) * quarter + lax.rem(s, quarter)
        src, dst = piece(gres, s, c), piece(pass_r.at[d], me - first, c)
        return other, src, dst, part_send.at[k, c], part_recv.at[d, me - first, c]

    def sum_out(d, c):
        return remote(
            far_sum.at[d, :, cols(c)], far_part.at[:, cols(c)], sum_send.at[d, c], sum_recv.at[c], source(d)
        )

    experts = base.shape[0]
    lower = (
        lax.broadcasted_iota(jnp.int32, (tok, tok), 0) < lax.broadcasted_iota(jnp.int32, (tok, tok), 1)
    ).astype(F32).astype(BF)

    def routing(words, begin, count):
        labels = lax.broadcasted_iota(jnp.int32, (experts, tok), 0)
        hits = [(words[k:k + 1] == labels).astype(F32) for k in range(chosen)]
        where = mm(functools.reduce(jnp.add, hits).astype(BF), lower) + base[...]
        slots = (lax.broadcasted_iota(jnp.int32, (count, tok), 0) + begin).astype(F32)
        marks = [(slots == jnp.sum(where * h, axis=0, keepdims=True)).astype(F32) for h in hits]
        code = [words[chosen + k:chosen + k + 1].astype(F32) for k in range(chosen)]
        total = functools.reduce(jnp.add, code)
        mix = functools.reduce(jnp.add, [m * (w / total) for m, w in zip(marks, code)])
        high = mix.astype(BF)
        low = (mix - high.astype(F32)).astype(BF)
        return functools.reduce(jnp.add, marks).astype(BF), high, low

    def combine(high, low, x):
        return mm(high, x, TN) + mm(low, x, TN)

    table[0], table[1], table[2] = routing(meta[...], 0, n * rows)
    own = pl.ds(pl.multiple_of(first * rows, 16), half * rows)

    def square(c, acc):
        v = hid[:, cols(c)].astype(F32)
        return acc + jnp.sum(v * v, axis=1, keepdims=True)

    zero = jnp.zeros((tok, 1), F32)
    scale = lax.rsqrt(lax.fori_loop(0, chunks, square, zero) / features + epsilon)

    @pl.loop(0, chunks)
    def _(c):
        v = (hid[:, cols(c)].astype(F32) * scale * gain[:, cols(c)]).astype(BF)
        send_n[:, cols(c)] = mm(table[0], v).astype(BF)
    start(0)

    @pl.loop(0, chunks)
    def _(c):
        og_out(c).start()

    @pl.loop(0, chunks)
    def _(c):
        send_g[:, cols(c)] = mm(table[0, own], og[:, cols(c)]).astype(BF)
    start(1)

    def forward_on(i):
        for j in range(nb):
            if j > 0:
                arrived(i, lax.rem(mb + j, nb) * nh + mh)
            for k in range(1, nh):
                to_head(i, j, k).start()

    def whole(i):
        keep_own(i).wait()
        for b in range(nb):
            for k in range(1, nh):
                arrived(i, b * nh + lax.rem(mh + k, nh))

    forward_on(0)
    forward_on(1)
    finish(0)
    whole(0)
    whole(1)
    gp[...] = jnp.zeros_like(gp)
    up[...] = jnp.zeros_like(up)

    @pl.loop(0, chunks)
    def _(c):
        x = recv_n[:, cols(c)]
        for e in range(local):
            xe = mm(pick[e], x).astype(BF)
            gp[e] += mm(xe, wg[c, e])
            up[e] += mm(xe, wu[c, e])

    @pl.when(relays)
    def _():
        for d in range(2):
            wait(far_meta.at[d], meta_sem.at[1 + d])
            far_table[d, 0], far_table[d, 1], far_table[d, 2] = routing(far_meta[d], first * rows, half * rows)

    def relay_grads(begin, end):
        @pl.when(relays)
        def _():
            @pl.loop(begin, end)
            def _(c):
                for d in range(2):
                    wait(far_og.at[d, :, cols(c)], og_sem.at[1 + d, c])
                    pass_g[d, :, cols(c)] = mm(far_table[d, 0], far_og[d, :, cols(c)]).astype(BF)

                    @pl.loop(1, half)
                    def _(k, d=d):
                        pass_on(d, k, c).start()
                    pltpu.make_async_copy(
                        piece(pass_g.at[d], me - first, c), piece(recv_g, source(d), c), r_sem.at[1, source(d)]
                    ).start()

    relay_grads(0, chunks // 2)
    forward_on(2)
    relay_grads(chunks // 2, chunks)
    whole(2)
    inner = [(jax.nn.silu(gp[e]) * up[e]).astype(BF) for e in range(local)]

    @pl.loop(0, chunks)
    def _(c):
        parts = [mm(place[e], mm(inner[e], wd[c, e]).astype(BF)) for e in range(local)]
        res[:, cols(c)] = functools.reduce(jnp.add, parts).astype(BF)
    start(2)

    finish(1)

    def back(c, acc):
        y = recv_g[:, cols(c)]
        return tuple(
            acc[e] + mm(mm(pick[e], y).astype(BF), wd[c, e], NT) for e in range(local)
        )

    none = tuple(jnp.zeros(gp.shape[1:], F32) for _ in range(local))
    grads = lax.fori_loop(0, chunks, back, none)
    g_gate, g_up = [], []
    for e in range(local):
        g = gp[e]
        s = jax.nn.sigmoid(g)
        g_gate.append((grads[e] * up[e] * s * (1.0 + g * (1.0 - s))).astype(BF))
        g_up.append((grads[e] * (g * s)).astype(BF))

    @pl.loop(0, chunks)
    def _(c):
        parts = []
        for e in range(local):
            r = mm(g_gate[e], wg[c, e], NT) + mm(g_up[e], wu[c, e], NT)
            parts.append(mm(place[e], r.astype(BF)))
        gres[:, cols(c)] = functools.reduce(jnp.add, parts).astype(BF)

        @pl.loop(0, half)
        def _(k):
            other, src, dst, send, recv = to_relay(k, c)

            @pl.when(other != me)
            def _():
                remote(src, dst, send, recv, other).start()

            @pl.when(other == me)
            def _():
                pltpu.make_async_copy(src, dst, recv).start()

        @pl.loop(1, half)
        def _(k):
            near_out(k, c).start()
        pltpu.make_async_copy(
            piece(gres, me, c), piece(gret, me - first, c), near_sem.at[1, me - first, c]
        ).start()

    def relay_sums(begin, end):
        @pl.when(relays)
        def _():
            @pl.loop(begin, end)
            def _(c):
                for d in range(2):
                    @pl.loop(0, half)
                    def _(j, d=d):
                        wait(piece(pass_r.at[d], j, c), part_recv.at[d, j, c])
                    x = pass_r[d, :, cols(c)]
                    far_sum[d, :, cols(c)] = combine(far_table[d, 1], far_table[d, 2], x).astype(BF)
                    sum_out(d, c).start()

    relay_sums(0, chunks // 2)
    finish(2)

    @pl.loop(0, chunks)
    def _(c):
        mixture = combine(table[1], table[2], ret[:, cols(c)])
        out[:, cols(c)] = (hid[:, cols(c)].astype(F32) + mixture).astype(BF)

    relay_sums(chunks // 2, chunks)

    def scaling(c, acc):
        @pl.loop(0, half)
        def _(j):
            wait(piece(gret, j, c), near_sem.at[1, j, c])
        wait(far_part.at[:, cols(c)], sum_recv.at[c])
        total = combine(table[1, own], table[2, own], gret[:, cols(c)]) + far_part[:, cols(c)].astype(F32)
        a = gain[:, cols(c)] * total
        scaled[:, cols(c)] = a
        return acc + jnp.sum(a * hid[:, cols(c)].astype(F32), axis=1, keepdims=True)

    mean = lax.fori_loop(0, chunks, scaling, zero) / features
    cubed = scale * scale * scale * mean

    @pl.loop(0, chunks)
    def _(c):
        gin[:, cols(c)] = (
            og[:, cols(c)].astype(F32) + scale * scaled[:, cols(c)] - hid[:, cols(c)].astype(F32) * cubed
        ).astype(BF)

    for step in range(3):
        @pl.loop(1, spans[step])
        def _(k, step=step):
            direct(step, k).wait_send()

    @pl.loop(0, chunks)
    def _(c):
        @pl.loop(0, half)
        def _(k):
            other, src, dst, send, recv = to_relay(k, c)

            @pl.when(other != me)
            def _():
                remote(src, dst, send, recv, other).wait_send()

        @pl.loop(1, half)
        def _(k):
            near_out(k, c).wait_send()
    meta_out().wait_send()

    @pl.loop(0, chunks)
    def _(c):
        og_out(c).wait_send()

    @pl.when(relays)
    def _():
        @pl.loop(0, chunks)
        def _(c):
            for d in range(2):
                @pl.loop(1, half)
                def _(k, d=d):
                    pass_on(d, k, c).wait_send()
                sum_out(d, c).wait_send()

    for i in range(3):
        @pl.loop(1, nb)
        def _(k, i=i):
            to_batch(i, k).wait_send()
        for j in range(nb):
            for k in range(1, nh):
                to_head(i, j, k).wait_send()


def body(hidden_in, norm_gain, w_gate, w_up, w_down, expert_ids, gate_codes, out_grad):
    n, nb, nh = (lax.axis_size(a) for a in ("expert", "batch", "head"))
    local, width, hidden = w_gate.shape
    experts = n * local
    tok, features = hidden_in.shape
    chosen = expert_ids.shape[1]
    cap = 3 * tok * chosen // (2 * experts)
    rows = -(-local * cap // 16) * 16
    chunks = nb * nh
    meta = jnp.concatenate([expert_ids, gate_codes], axis=1).T
    meta = jnp.pad(meta, ((0, -2 * chosen % 8), (0, 0)))
    numbers = np.arange(experts)
    base = (numbers // local * rows + numbers % local * cap).astype(np.float32)[:, None]
    pick = np.zeros((local, n * cap, n * rows), np.float32)
    for e in range(local):
        line = np.arange(n * cap)
        pick[e, line, line // cap * rows + e * cap + line % cap] = 1.0
    place = pick.transpose(0, 2, 1)
    flow = pltpu.VMEM((n * rows, features), BF)
    vmem = pl.BlockSpec(memory_space=pltpu.VMEM)
    hbm = pl.BlockSpec(memory_space=pl.ANY)
    dma = pltpu.SemaphoreType.DMA
    out_type = jax.ShapeDtypeStruct((tok, features), BF)
    return pl.pallas_call(
        functools.partial(kernel, (n, nb, nh, cap, rows, local, chosen)),
        out_shape=(out_type, out_type),
        in_specs=[vmem, vmem, hbm, hbm, hbm] + [vmem] * 5,
        out_specs=(vmem, vmem),
        scratch_shapes=[
            pltpu.VMEM((chunks, local, width, hidden), BF),
            pltpu.VMEM((chunks, local, width, hidden), BF),
            pltpu.VMEM((chunks, local, hidden, width), BF),
        ] + [flow] * 6 + [
            pltpu.VMEM((n // 2 * rows, features), BF),
            pltpu.VMEM((n // 2 * rows, features), BF),
            pltpu.VMEM((2, n // 2 * rows, features), BF),
            pltpu.VMEM((2, n // 2 * rows, features), BF),
            pltpu.VMEM((2, tok, features), BF),
            pltpu.VMEM((tok, features), BF),
            pltpu.VMEM((2, tok, features), BF),
            pltpu.VMEM((2,) + meta.shape, jnp.int32),
            pltpu.VMEM((2, 3, n // 2 * rows, tok), BF),
            pltpu.VMEM((local, n * cap, hidden), F32),
            pltpu.VMEM((local, n * cap, hidden), F32),
            pltpu.VMEM((tok, features), F32),
            pltpu.VMEM((3, n * rows, tok), BF),
            dma((3, n)), dma((3, n)), dma((2, n // 2, chunks)), dma((2, n // 2, chunks)),
            dma((n // 2, chunks)), dma((2, n // 2, chunks)), dma((3, chunks)), dma((2, chunks)), dma((chunks,)),
            dma((3,)),
            dma((3, nb)), dma((3, nb, nh)), dma((3, chunks)), dma((3,)),
        ],
        compiler_params=pltpu.CompilerParams(
            collective_id=0, has_side_effects=True, vmem_limit_bytes=60 * 1024 * 1024
        ),
    )(
        hidden_in, norm_gain[None], w_gate, w_up, w_down, meta, out_grad,
        jnp.asarray(base), jnp.asarray(pick, BF), jnp.asarray(place, BF),
    )


def solution(mesh):
    tokens = P(("batch", "head", "expert"), None)
    in_specs = (
        tokens,
        P(),
        P("expert", ("batch", "head"), None),
        P("expert", ("batch", "head"), None),
        P("expert", None, ("batch", "head")),
        tokens,
        tokens,
        tokens,
    )
    return jax.shard_map(body, mesh=mesh, in_specs=in_specs, out_specs=(tokens, tokens), check_vma=False)
```

```python
import functools

import jax
import jax.numpy as jnp
import numpy as np
from jax import lax
from jax.experimental import pallas as pl
from jax.experimental.pallas import tpu as pltpu
from jax.sharding import PartitionSpec as P

epsilon = 1e-06
MESH = pl.DeviceIdType.MESH
BF = jnp.bfloat16
F32 = jnp.float32
NN = (((1,), (0,)), ((), ()))
NT = (((1,), (1,)), ((), ()))
TN = (((0,), (0,)), ((), ()))


def mm(a, b, dims=NN):
    return lax.dot_general(a, b, dims, preferred_element_type=F32)


def kernel(
    sizes, hid, gain, wg_in, wu_in, wd_in, meta, og, base, pick, place, out, gin,
    wg, wu, wd, send_n, recv_n, recv_g, res, gres, ret, send_g, gret, pass_g, pass_r,
    far_og, far_part, far_sum, far_meta, far_table, gp, up, scaled, table,
    s_sem, r_sem, near_sem, pass_send, part_send, part_recv, og_sem, sum_send, sum_recv, meta_sem, wb_send, wh_send, w_recv, w_own,
):
    n, nb, nh, cap, rows, local, chosen = sizes
    me, mb, mh = (lax.axis_index(a) for a in ("expert", "batch", "head"))
    tok, features = hid.shape
    chunks = nb * nh
    width = features // chunks
    mine = mb * nh + mh
    peers = (("expert", me, n), ("batch", mb, nb), ("head", mh, nh))

    barrier = pltpu.get_barrier_semaphore()
    for axis, at, count in peers:
        @pl.loop(1, count)
        def _(k, axis=axis, at=at, count=count):
            pl.semaphore_signal(
                barrier, inc=1, device_id={axis: lax.rem(at + k, count)}, device_id_type=MESH
            )
    pl.semaphore_wait(barrier, n + nb + nh - 3)

    tensors = ((wg_in, wg), (wu_in, wu), (wd_in, wd))

    def to_batch(i, k):
        src, dst = tensors[i]
        other = lax.rem(mb + k, nb)
        return pltpu.make_async_remote_copy(
            src_ref=src, dst_ref=dst.at[mine], send_sem=wb_send.at[i, k], recv_sem=w_recv.at[i, mine],
            device_id={"batch": other}, device_id_type=MESH,
        )

    def to_head(i, j, k):
        src, dst = tensors[i]
        b = lax.rem(mb + j, nb)
        slot = b * nh + mh
        return pltpu.make_async_remote_copy(
            src_ref=src if j == 0 else dst.at[slot], dst_ref=dst.at[slot],
            send_sem=wh_send.at[i, j, k], recv_sem=w_recv.at[i, slot],
            device_id={"head": lax.rem(mh + k, nh)}, device_id_type=MESH,
        )

    def arrived(i, slot):
        dst = tensors[i][1].at[slot]
        pltpu.make_async_copy(dst, dst, w_recv.at[i, slot]).wait()

    def keep_own(i):
        return pltpu.make_async_copy(tensors[i][0], tensors[i][1].at[mine], w_own.at[i])

    quarter, half = n // 4, n // 2
    side, lane, q = me // half, lax.rem(me, quarter), me // quarter
    first = side * half
    relays = q == 1 + side
    turn = (1 - side) * (1 - q) + side * (q - 2)
    beyond = (2 - side) * quarter + lane

    def cols(c):
        return pl.ds(pl.multiple_of(c * width, 128), width)

    def source(d):
        return ((2 - side) + d * (1 - 2 * side)) * quarter + lane

    def remote(src, dst, send, recv, other):
        return pltpu.make_async_remote_copy(
            src_ref=src, dst_ref=dst, send_sem=send, recv_sem=recv,
            device_id={"expert": other}, device_id_type=MESH,
        )

    def meta_out():
        return remote(meta, far_meta.at[turn], meta_sem.at[0], meta_sem.at[1 + turn], beyond)

    def og_out(c):
        return remote(
            og.at[:, cols(c)], far_og.at[turn, :, cols(c)], og_sem.at[0, c], og_sem.at[1 + turn, c], beyond
        )

    def wait(ref, sem):
        pltpu.make_async_copy(ref, ref, sem).wait()

    early = chunks // 4
    meta_out().start()

    @pl.loop(0, early)
    def _(c):
        og_out(c).start()
    for i in range(3):
        @pl.loop(1, nb)
        def _(k, i=i):
            to_batch(i, k).start()
        keep_own(i).start()

    def block(ref, d):
        return ref.at[pl.ds(pl.multiple_of(d * rows, 16), rows)]

    def near(k):
        return first + lax.rem(me - first + k, half)

    def direct(step, k):
        other = near(k)
        if step == 1:
            src, dst = block(send_g, other - first), block(recv_g, me)
        else:
            other = lax.rem(me + 1 + lax.rem(k + half - 2, n - 1), n)
            src, dst = ((send_n, recv_n), None, (res, ret))[step]
            src, dst = block(src, other), block(dst, me)
        return remote(src, dst, s_sem.at[step, other], r_sem.at[step, me], other)

    homes = ((send_n, recv_n), (send_g, recv_g), (res, ret))
    spans = (n, half, n)

    def start(step):
        @pl.loop(1, spans[step])
        def _(k):
            direct(step, k).start()
        src, dst = homes[step]
        at = me - first if step == 1 else me
        pltpu.make_async_copy(block(src, at), block(dst, me), r_sem.at[step, me]).start()

    def finish(step):
        dst = homes[step][1]

        @pl.loop(0, n)
        def _(j):
            wait(block(dst, j), r_sem.at[step, j])

    def piece(ref, j, c):
        return ref.at[pl.ds(pl.multiple_of(j * rows, 16), rows), cols(c)]

    def near_out(k, c):
        other = near(k)
        return remote(
            piece(gres, other, c), piece(gret, me - first, c),
            near_sem.at[0, k, c], near_sem.at[1, me - first, c], other,
        )

    def pass_on(d, k, c):
        other = near(k)
        return remote(
            piece(pass_g.at[d], other - first, c), piece(recv_g, source(d), c),
            pass_send.at[d, k, c], r_sem.at[1, source(d)], other,
        )

    def to_relay(k, c):
        s = half - first + k
        qs = s // quarter
        d = side * (1 - qs) + (1 - side) * (qs - 2)
        other = (1 + side) * quarter + lax.rem(s, quarter)
        src, dst = piece(gres, s, c), piece(pass_r.at[d], me - first, c)
        return other, src, dst, part_send.at[k, c], part_recv.at[d, me - first, c]

    def sum_out(d, c):
        return remote(
            far_sum.at[d, :, cols(c)], far_part.at[:, cols(c)], sum_send.at[d, c], sum_recv.at[c], source(d)
        )

    experts = base.shape[0]
    lower = (
        lax.broadcasted_iota(jnp.int32, (tok, tok), 0) < lax.broadcasted_iota(jnp.int32, (tok, tok), 1)
    ).astype(F32).astype(BF)

    def routing(words, begin, count):
        labels = lax.broadcasted_iota(jnp.int32, (experts, tok), 0)
        hits = [(words[k:k + 1] == labels).astype(F32) for k in range(chosen)]
        where = mm(functools.reduce(jnp.add, hits).astype(BF), lower) + base[...]
        slots = (lax.broadcasted_iota(jnp.int32, (count, tok), 0) + begin).astype(F32)
        marks = [(slots == jnp.sum(where * h, axis=0, keepdims=True)).astype(F32) for h in hits]
        code = [words[chosen + k:chosen + k + 1].astype(F32) for k in range(chosen)]
        total = functools.reduce(jnp.add, code)
        mix = functools.reduce(jnp.add, [m * (w / total) for m, w in zip(marks, code)])
        high = mix.astype(BF)
        low = (mix - high.astype(F32)).astype(BF)
        return functools.reduce(jnp.add, marks).astype(BF), high, low

    def combine(high, low, x):
        return mm(high, x, TN) + mm(low, x, TN)

    table[0], table[1], table[2] = routing(meta[...], 0, n * rows)
    own = pl.ds(pl.multiple_of(first * rows, 16), half * rows)

    def square(c, acc):
        v = hid[:, cols(c)].astype(F32)
        return acc + jnp.sum(v * v, axis=1, keepdims=True)

    zero = jnp.zeros((tok, 1), F32)
    scale = lax.rsqrt(lax.fori_loop(0, chunks, square, zero) / features + epsilon)

    @pl.loop(0, chunks)
    def _(c):
        v = (hid[:, cols(c)].astype(F32) * scale * gain[:, cols(c)]).astype(BF)
        send_n[:, cols(c)] = mm(table[0], v).astype(BF)
    start(0)

    @pl.loop(early, chunks)
    def _(c):
        og_out(c).start()

    @pl.loop(0, chunks)
    def _(c):
        send_g[:, cols(c)] = mm(table[0, own], og[:, cols(c)]).astype(BF)
    start(1)

    def forward_on(i):
        for j in range(nb):
            if j > 0:
                arrived(i, lax.rem(mb + j, nb) * nh + mh)
            for k in range(1, nh):
                to_head(i, j, k).start()

    def whole(i):
        keep_own(i).wait()
        for b in range(nb):
            for k in range(1, nh):
                arrived(i, b * nh + lax.rem(mh + k, nh))

    forward_on(0)
    forward_on(1)
    finish(0)
    whole(0)
    whole(1)
    gp[...] = jnp.zeros_like(gp)
    up[...] = jnp.zeros_like(up)

    @pl.loop(0, chunks)
    def _(c):
        x = recv_n[:, cols(c)]
        for e in range(local):
            xe = mm(pick[e], x).astype(BF)
            gp[e] += mm(xe, wg[c, e])
            up[e] += mm(xe, wu[c, e])

    @pl.when(relays)
    def _():
        for d in range(2):
            wait(far_meta.at[d], meta_sem.at[1 + d])
            far_table[d, 0], far_table[d, 1], far_table[d, 2] = routing(far_meta[d], first * rows, half * rows)

    def relay_grads(begin, end):
        @pl.when(relays)
        def _():
            @pl.loop(begin, end)
            def _(c):
                for d in range(2):
                    wait(far_og.at[d, :, cols(c)], og_sem.at[1 + d, c])
                    pass_g[d, :, cols(c)] = mm(far_table[d, 0], far_og[d, :, cols(c)]).astype(BF)

                    @pl.loop(1, half)
                    def _(k, d=d):
                        pass_on(d, k, c).start()
                    pltpu.make_async_copy(
                        piece(pass_g.at[d], me - first, c), piece(recv_g, source(d), c), r_sem.at[1, source(d)]
                    ).start()

    relay_grads(0, chunks // 2)
    forward_on(2)
    relay_grads(chunks // 2, chunks)
    whole(2)
    inner = [(jax.nn.silu(gp[e]) * up[e]).astype(BF) for e in range(local)]

    @pl.loop(0, chunks)
    def _(c):
        parts = [mm(place[e], mm(inner[e], wd[c, e]).astype(BF)) for e in range(local)]
        res[:, cols(c)] = functools.reduce(jnp.add, parts).astype(BF)
    start(2)

    finish(1)

    def back(c, acc):
        y = recv_g[:, cols(c)]
        return tuple(
            acc[e] + mm(mm(pick[e], y).astype(BF), wd[c, e], NT) for e in range(local)
        )

    none = tuple(jnp.zeros(gp.shape[1:], F32) for _ in range(local))
    grads = lax.fori_loop(0, chunks, back, none)
    g_gate, g_up = [], []
    for e in range(local):
        g = gp[e]
        s = jax.nn.sigmoid(g)
        g_gate.append((grads[e] * up[e] * s * (1.0 + g * (1.0 - s))).astype(BF))
        g_up.append((grads[e] * (g * s)).astype(BF))

    @pl.loop(0, chunks)
    def _(c):
        parts = []
        for e in range(local):
            r = mm(g_gate[e], wg[c, e], NT) + mm(g_up[e], wu[c, e], NT)
            parts.append(mm(place[e], r.astype(BF)))
        gres[:, cols(c)] = functools.reduce(jnp.add, parts).astype(BF)

        @pl.loop(0, half)
        def _(k):
            other, src, dst, send, recv = to_relay(k, c)

            @pl.when(other != me)
            def _():
                remote(src, dst, send, recv, other).start()

            @pl.when(other == me)
            def _():
                pltpu.make_async_copy(src, dst, recv).start()

        @pl.loop(1, half)
        def _(k):
            near_out(k, c).start()
        pltpu.make_async_copy(
            piece(gres, me, c), piece(gret, me - first, c), near_sem.at[1, me - first, c]
        ).start()

    def relay_sums(begin, end):
        @pl.when(relays)
        def _():
            @pl.loop(begin, end)
            def _(c):
                for d in range(2):
                    @pl.loop(0, half)
                    def _(j, d=d):
                        wait(piece(pass_r.at[d], j, c), part_recv.at[d, j, c])
                    x = pass_r[d, :, cols(c)]
                    far_sum[d, :, cols(c)] = combine(far_table[d, 1], far_table[d, 2], x).astype(BF)
                    sum_out(d, c).start()

    relay_sums(0, chunks // 2)
    finish(2)

    @pl.loop(0, chunks)
    def _(c):
        mixture = combine(table[1], table[2], ret[:, cols(c)])
        out[:, cols(c)] = (hid[:, cols(c)].astype(F32) + mixture).astype(BF)

    relay_sums(chunks // 2, chunks)

    def scaling(c, acc):
        @pl.loop(0, half)
        def _(j):
            wait(piece(gret, j, c), near_sem.at[1, j, c])
        wait(far_part.at[:, cols(c)], sum_recv.at[c])
        total = combine(table[1, own], table[2, own], gret[:, cols(c)]) + far_part[:, cols(c)].astype(F32)
        a = gain[:, cols(c)] * total
        scaled[:, cols(c)] = a
        return acc + jnp.sum(a * hid[:, cols(c)].astype(F32), axis=1, keepdims=True)

    mean = lax.fori_loop(0, chunks, scaling, zero) / features
    cubed = scale * scale * scale * mean

    @pl.loop(0, chunks)
    def _(c):
        gin[:, cols(c)] = (
            og[:, cols(c)].astype(F32) + scale * scaled[:, cols(c)] - hid[:, cols(c)].astype(F32) * cubed
        ).astype(BF)

    for step in range(3):
        @pl.loop(1, spans[step])
        def _(k, step=step):
            direct(step, k).wait_send()

    @pl.loop(0, chunks)
    def _(c):
        @pl.loop(0, half)
        def _(k):
            other, src, dst, send, recv = to_relay(k, c)

            @pl.when(other != me)
            def _():
                remote(src, dst, send, recv, other).wait_send()

        @pl.loop(1, half)
        def _(k):
            near_out(k, c).wait_send()
    meta_out().wait_send()

    @pl.loop(0, chunks)
    def _(c):
        og_out(c).wait_send()

    @pl.when(relays)
    def _():
        @pl.loop(0, chunks)
        def _(c):
            for d in range(2):
                @pl.loop(1, half)
                def _(k, d=d):
                    pass_on(d, k, c).wait_send()
                sum_out(d, c).wait_send()

    for i in range(3):
        @pl.loop(1, nb)
        def _(k, i=i):
            to_batch(i, k).wait_send()
        for j in range(nb):
            for k in range(1, nh):
                to_head(i, j, k).wait_send()


def body(hidden_in, norm_gain, w_gate, w_up, w_down, expert_ids, gate_codes, out_grad):
    n, nb, nh = (lax.axis_size(a) for a in ("expert", "batch", "head"))
    local, width, hidden = w_gate.shape
    experts = n * local
    tok, features = hidden_in.shape
    chosen = expert_ids.shape[1]
    cap = 3 * tok * chosen // (2 * experts)
    rows = -(-local * cap // 16) * 16
    chunks = nb * nh
    meta = jnp.concatenate([expert_ids, gate_codes], axis=1).T
    meta = jnp.pad(meta, ((0, -2 * chosen % 8), (0, 0)))
    numbers = np.arange(experts)
    base = (numbers // local * rows + numbers % local * cap).astype(np.float32)[:, None]
    pick = np.zeros((local, n * cap, n * rows), np.float32)
    for e in range(local):
        line = np.arange(n * cap)
        pick[e, line, line // cap * rows + e * cap + line % cap] = 1.0
    place = pick.transpose(0, 2, 1)
    flow = pltpu.VMEM((n * rows, features), BF)
    vmem = pl.BlockSpec(memory_space=pltpu.VMEM)
    hbm = pl.BlockSpec(memory_space=pl.ANY)
    dma = pltpu.SemaphoreType.DMA
    out_type = jax.ShapeDtypeStruct((tok, features), BF)
    return pl.pallas_call(
        functools.partial(kernel, (n, nb, nh, cap, rows, local, chosen)),
        out_shape=(out_type, out_type),
        in_specs=[vmem, vmem, hbm, hbm, hbm] + [vmem] * 5,
        out_specs=(vmem, vmem),
        scratch_shapes=[
            pltpu.VMEM((chunks, local, width, hidden), BF),
            pltpu.VMEM((chunks, local, width, hidden), BF),
            pltpu.VMEM((chunks, local, hidden, width), BF),
        ] + [flow] * 6 + [
            pltpu.VMEM((n // 2 * rows, features), BF),
            pltpu.VMEM((n // 2 * rows, features), BF),
            pltpu.VMEM((2, n // 2 * rows, features), BF),
            pltpu.VMEM((2, n // 2 * rows, features), BF),
            pltpu.VMEM((2, tok, features), BF),
            pltpu.VMEM((tok, features), BF),
            pltpu.VMEM((2, tok, features), BF),
            pltpu.VMEM((2,) + meta.shape, jnp.int32),
            pltpu.VMEM((2, 3, n // 2 * rows, tok), BF),
            pltpu.VMEM((local, n * cap, hidden), F32),
            pltpu.VMEM((local, n * cap, hidden), F32),
            pltpu.VMEM((tok, features), F32),
            pltpu.VMEM((3, n * rows, tok), BF),
            dma((3, n)), dma((3, n)), dma((2, n // 2, chunks)), dma((2, n // 2, chunks)),
            dma((n // 2, chunks)), dma((2, n // 2, chunks)), dma((3, chunks)), dma((2, chunks)), dma((chunks,)),
            dma((3,)),
            dma((3, nb)), dma((3, nb, nh)), dma((3, chunks)), dma((3,)),
        ],
        compiler_params=pltpu.CompilerParams(
            collective_id=0, has_side_effects=True, vmem_limit_bytes=60 * 1024 * 1024
        ),
    )(
        hidden_in, norm_gain[None], w_gate, w_up, w_down, meta, out_grad,
        jnp.asarray(base), jnp.asarray(pick, BF), jnp.asarray(place, BF),
    )


def solution(mesh):
    tokens = P(("batch", "head", "expert"), None)
    in_specs = (
        tokens,
        P(),
        P("expert", ("batch", "head"), None),
        P("expert", ("batch", "head"), None),
        P("expert", None, ("batch", "head")),
        tokens,
        tokens,
        tokens,
    )
    return jax.shard_map(body, mesh=mesh, in_specs=in_specs, out_specs=(tokens, tokens), check_vma=False)
```

```python
import functools

import jax
import jax.numpy as jnp
import numpy as np
from jax import lax
from jax.experimental import pallas as pl
from jax.experimental.pallas import tpu as pltpu
from jax.sharding import PartitionSpec as P

epsilon = 1e-06
MESH = pl.DeviceIdType.MESH
BF = jnp.bfloat16
F32 = jnp.float32
NN = (((1,), (0,)), ((), ()))
NT = (((1,), (1,)), ((), ()))
TN = (((0,), (0,)), ((), ()))


def mm(a, b, dims=NN):
    return lax.dot_general(a, b, dims, preferred_element_type=F32)


def kernel(
    sizes, hid, gain, wg_in, wu_in, wd_in, meta, og, base, pick, place, out, gin,
    wg, wu, wd, send_n, recv_n, recv_g, res, gres, ret, send_g, gret, pass_g, pass_r,
    far_og, far_part, far_sum, far_meta, far_table, gp, up, scaled, table,
    s_sem, r_sem, near_sem, pass_send, part_send, part_recv, og_sem, sum_send, sum_recv, meta_sem, wb_send, wh_send, w_recv, w_own,
):
    n, nb, nh, cap, rows, local, chosen = sizes
    me, mb, mh = (lax.axis_index(a) for a in ("expert", "batch", "head"))
    tok, features = hid.shape
    chunks = nb * nh
    width = features // chunks
    mine = mb * nh + mh
    peers = (("expert", me, n), ("batch", mb, nb), ("head", mh, nh))

    barrier = pltpu.get_barrier_semaphore()
    for axis, at, count in peers:
        @pl.loop(1, count)
        def _(k, axis=axis, at=at, count=count):
            pl.semaphore_signal(
                barrier, inc=1, device_id={axis: lax.rem(at + k, count)}, device_id_type=MESH
            )
    pl.semaphore_wait(barrier, n + nb + nh - 3)

    tensors = ((wg_in, wg), (wu_in, wu), (wd_in, wd))

    def to_batch(i, k):
        src, dst = tensors[i]
        other = lax.rem(mb + k, nb)
        return pltpu.make_async_remote_copy(
            src_ref=src, dst_ref=dst.at[mine], send_sem=wb_send.at[i, k], recv_sem=w_recv.at[i, mine],
            device_id={"batch": other}, device_id_type=MESH,
        )

    def to_head(i, j, k):
        src, dst = tensors[i]
        b = lax.rem(mb + j, nb)
        slot = b * nh + mh
        return pltpu.make_async_remote_copy(
            src_ref=src if j == 0 else dst.at[slot], dst_ref=dst.at[slot],
            send_sem=wh_send.at[i, j, k], recv_sem=w_recv.at[i, slot],
            device_id={"head": lax.rem(mh + k, nh)}, device_id_type=MESH,
        )

    def arrived(i, slot):
        dst = tensors[i][1].at[slot]
        pltpu.make_async_copy(dst, dst, w_recv.at[i, slot]).wait()

    def keep_own(i):
        return pltpu.make_async_copy(tensors[i][0], tensors[i][1].at[mine], w_own.at[i])

    quarter, half = n // 4, n // 2
    side, lane, q = me // half, lax.rem(me, quarter), me // quarter
    first = side * half
    relays = q == 1 + side
    turn = (1 - side) * (1 - q) + side * (q - 2)
    beyond = (2 - side) * quarter + lane

    def cols(c):
        return pl.ds(pl.multiple_of(c * width, 128), width)

    def source(d):
        return ((2 - side) + d * (1 - 2 * side)) * quarter + lane

    def remote(src, dst, send, recv, other):
        return pltpu.make_async_remote_copy(
            src_ref=src, dst_ref=dst, send_sem=send, recv_sem=recv,
            device_id={"expert": other}, device_id_type=MESH,
        )

    def meta_out():
        return remote(meta, far_meta.at[turn], meta_sem.at[0], meta_sem.at[1 + turn], beyond)

    def og_out(c):
        return remote(
            og.at[:, cols(c)], far_og.at[turn, :, cols(c)], og_sem.at[0, c], og_sem.at[1 + turn, c], beyond
        )

    def wait(ref, sem):
        pltpu.make_async_copy(ref, ref, sem).wait()

    early = chunks // 4
    meta_out().start()

    @pl.loop(0, early)
    def _(c):
        og_out(c).start()
    for i in range(3):
        @pl.loop(1, nb)
        def _(k, i=i):
            to_batch(i, k).start()
        keep_own(i).start()

    def block(ref, d):
        return ref.at[pl.ds(pl.multiple_of(d * rows, 16), rows)]

    def near(k):
        return first + lax.rem(me - first + k, half)

    def direct(step, k, c=None):
        other = near(k)
        if step == 1:
            src, dst = block(send_g, other - first), block(recv_g, me)
        else:
            other = lax.rem(me + 1 + lax.rem(k + half - 2, n - 1), n)
            src, dst = ((send_n, recv_n), None, (res, ret))[step]
            src, dst = block(src, other), block(dst, me)
        if c is not None:
            src, dst = src.at[:, cols(c)], dst.at[:, cols(c)]
        return remote(src, dst, s_sem.at[step, other], r_sem.at[step, me], other)

    homes = ((send_n, recv_n), (send_g, recv_g), (res, ret))
    spans = (n, half, n)

    def stream(step, c):
        @pl.loop(1, spans[step])
        def _(k):
            direct(step, k, c).start()

    def keep(step):
        src, dst = homes[step]
        at = me - first if step == 1 else me
        pltpu.make_async_copy(block(src, at), block(dst, me), r_sem.at[step, me]).start()

    def finish(step):
        dst = homes[step][1]

        @pl.loop(0, n)
        def _(j):
            wait(block(dst, j), r_sem.at[step, j])

    def piece(ref, j, c):
        return ref.at[pl.ds(pl.multiple_of(j * rows, 16), rows), cols(c)]

    def near_out(k, c):
        other = near(k)
        return remote(
            piece(gres, other, c), piece(gret, me - first, c),
            near_sem.at[0, k, c], near_sem.at[1, me - first, c], other,
        )

    def pass_on(d, k, c):
        other = near(k)
        return remote(
            piece(pass_g.at[d], other - first, c), piece(recv_g, source(d), c),
            pass_send.at[d, k, c], r_sem.at[1, source(d)], other,
        )

    def to_relay(k, c):
        s = half - first + k
        qs = s // quarter
        d = side * (1 - qs) + (1 - side) * (qs - 2)
        other = (1 + side) * quarter + lax.rem(s, quarter)
        src, dst = piece(gres, s, c), piece(pass_r.at[d], me - first, c)
        return other, src, dst, part_send.at[k, c], part_recv.at[d, me - first, c]

    def sum_out(d, c):
        return remote(
            far_sum.at[d, :, cols(c)], far_part.at[:, cols(c)], sum_send.at[d, c], sum_recv.at[c], source(d)
        )

    experts = base.shape[0]
    lower = (
        lax.broadcasted_iota(jnp.int32, (tok, tok), 0) < lax.broadcasted_iota(jnp.int32, (tok, tok), 1)
    ).astype(F32).astype(BF)

    def routing(words, begin, count):
        labels = lax.broadcasted_iota(jnp.int32, (experts, tok), 0)
        hits = [(words[k:k + 1] == labels).astype(F32) for k in range(chosen)]
        where = mm(functools.reduce(jnp.add, hits).astype(BF), lower) + base[...]
        slots = (lax.broadcasted_iota(jnp.int32, (count, tok), 0) + begin).astype(F32)
        marks = [(slots == jnp.sum(where * h, axis=0, keepdims=True)).astype(F32) for h in hits]
        code = [words[chosen + k:chosen + k + 1].astype(F32) for k in range(chosen)]
        total = functools.reduce(jnp.add, code)
        mix = functools.reduce(jnp.add, [m * (w / total) for m, w in zip(marks, code)])
        high = mix.astype(BF)
        low = (mix - high.astype(F32)).astype(BF)
        return functools.reduce(jnp.add, marks).astype(BF), high, low

    def combine(high, low, x):
        return mm(high, x, TN) + mm(low, x, TN)

    table[0], table[1], table[2] = routing(meta[...], 0, n * rows)
    own = pl.ds(pl.multiple_of(first * rows, 16), half * rows)

    def square(c, acc):
        v = hid[:, cols(c)].astype(F32)
        return acc + jnp.sum(v * v, axis=1, keepdims=True)

    zero = jnp.zeros((tok, 1), F32)
    scale = lax.rsqrt(lax.fori_loop(0, chunks, square, zero) / features + epsilon)

    @pl.loop(0, chunks)
    def _(c):
        v = (hid[:, cols(c)].astype(F32) * scale * gain[:, cols(c)]).astype(BF)
        send_n[:, cols(c)] = mm(table[0], v).astype(BF)
        stream(0, c)
    keep(0)

    @pl.loop(early, chunks)
    def _(c):
        og_out(c).start()

    @pl.loop(0, chunks)
    def _(c):
        send_g[:, cols(c)] = mm(table[0, own], og[:, cols(c)]).astype(BF)
        stream(1, c)
    keep(1)

    def forward_on(i):
        for j in range(nb):
            if j > 0:
                arrived(i, lax.rem(mb + j, nb) * nh + mh)
            for k in range(1, nh):
                to_head(i, j, k).start()

    def whole(i):
        keep_own(i).wait()
        for b in range(nb):
            for k in range(1, nh):
                arrived(i, b * nh + lax.rem(mh + k, nh))

    forward_on(0)
    forward_on(1)
    finish(0)
    whole(0)
    whole(1)
    gp[...] = jnp.zeros_like(gp)
    up[...] = jnp.zeros_like(up)

    @pl.loop(0, chunks)
    def _(c):
        x = recv_n[:, cols(c)]
        for e in range(local):
            xe = mm(pick[e], x).astype(BF)
            gp[e] += mm(xe, wg[c, e])
            up[e] += mm(xe, wu[c, e])

    @pl.when(relays)
    def _():
        for d in range(2):
            wait(far_meta.at[d], meta_sem.at[1 + d])
            far_table[d, 0], far_table[d, 1], far_table[d, 2] = routing(far_meta[d], first * rows, half * rows)

    def relay_grads(begin, end):
        @pl.when(relays)
        def _():
            @pl.loop(begin, end)
            def _(c):
                for d in range(2):
                    wait(far_og.at[d, :, cols(c)], og_sem.at[1 + d, c])
                    pass_g[d, :, cols(c)] = mm(far_table[d, 0], far_og[d, :, cols(c)]).astype(BF)

                    @pl.loop(1, half)
                    def _(k, d=d):
                        pass_on(d, k, c).start()
                    pltpu.make_async_copy(
                        piece(pass_g.at[d], me - first, c), piece(recv_g, source(d), c), r_sem.at[1, source(d)]
                    ).start()

    relay_grads(0, chunks // 2)
    forward_on(2)
    relay_grads(chunks // 2, chunks)
    whole(2)
    inner = [(jax.nn.silu(gp[e]) * up[e]).astype(BF) for e in range(local)]

    @pl.loop(0, chunks)
    def _(c):
        parts = [mm(place[e], mm(inner[e], wd[c, e]).astype(BF)) for e in range(local)]
        res[:, cols(c)] = functools.reduce(jnp.add, parts).astype(BF)
        stream(2, c)
    keep(2)

    finish(1)

    def back(c, acc):
        y = recv_g[:, cols(c)]
        return tuple(
            acc[e] + mm(mm(pick[e], y).astype(BF), wd[c, e], NT) for e in range(local)
        )

    none = tuple(jnp.zeros(gp.shape[1:], F32) for _ in range(local))
    grads = lax.fori_loop(0, chunks, back, none)
    g_gate, g_up = [], []
    for e in range(local):
        g = gp[e]
        s = jax.nn.sigmoid(g)
        g_gate.append((grads[e] * up[e] * s * (1.0 + g * (1.0 - s))).astype(BF))
        g_up.append((grads[e] * (g * s)).astype(BF))

    @pl.loop(0, chunks)
    def _(c):
        parts = []
        for e in range(local):
            r = mm(g_gate[e], wg[c, e], NT) + mm(g_up[e], wu[c, e], NT)
            parts.append(mm(place[e], r.astype(BF)))
        gres[:, cols(c)] = functools.reduce(jnp.add, parts).astype(BF)

        @pl.loop(0, half)
        def _(k):
            other, src, dst, send, recv = to_relay(k, c)

            @pl.when(other != me)
            def _():
                remote(src, dst, send, recv, other).start()

            @pl.when(other == me)
            def _():
                pltpu.make_async_copy(src, dst, recv).start()

        @pl.loop(1, half)
        def _(k):
            near_out(k, c).start()
        pltpu.make_async_copy(
            piece(gres, me, c), piece(gret, me - first, c), near_sem.at[1, me - first, c]
        ).start()

    def relay_sums(begin, end):
        @pl.when(relays)
        def _():
            @pl.loop(begin, end)
            def _(c):
                for d in range(2):
                    @pl.loop(0, half)
                    def _(j, d=d):
                        wait(piece(pass_r.at[d], j, c), part_recv.at[d, j, c])
                    x = pass_r[d, :, cols(c)]
                    far_sum[d, :, cols(c)] = combine(far_table[d, 1], far_table[d, 2], x).astype(BF)
                    sum_out(d, c).start()

    relay_sums(0, chunks // 2)
    finish(2)

    @pl.loop(0, chunks)
    def _(c):
        mixture = combine(table[1], table[2], ret[:, cols(c)])
        out[:, cols(c)] = (hid[:, cols(c)].astype(F32) + mixture).astype(BF)

    relay_sums(chunks // 2, chunks)

    def scaling(c, acc):
        @pl.loop(0, half)
        def _(j):
            wait(piece(gret, j, c), near_sem.at[1, j, c])
        wait(far_part.at[:, cols(c)], sum_recv.at[c])
        total = combine(table[1, own], table[2, own], gret[:, cols(c)]) + far_part[:, cols(c)].astype(F32)
        a = gain[:, cols(c)] * total
        scaled[:, cols(c)] = a
        return acc + jnp.sum(a * hid[:, cols(c)].astype(F32), axis=1, keepdims=True)

    mean = lax.fori_loop(0, chunks, scaling, zero) / features
    cubed = scale * scale * scale * mean

    @pl.loop(0, chunks)
    def _(c):
        gin[:, cols(c)] = (
            og[:, cols(c)].astype(F32) + scale * scaled[:, cols(c)] - hid[:, cols(c)].astype(F32) * cubed
        ).astype(BF)

    for step in range(3):
        @pl.loop(1, spans[step])
        def _(k, step=step):
            direct(step, k).wait_send()

    @pl.loop(0, chunks)
    def _(c):
        @pl.loop(0, half)
        def _(k):
            other, src, dst, send, recv = to_relay(k, c)

            @pl.when(other != me)
            def _():
                remote(src, dst, send, recv, other).wait_send()

        @pl.loop(1, half)
        def _(k):
            near_out(k, c).wait_send()
    meta_out().wait_send()

    @pl.loop(0, chunks)
    def _(c):
        og_out(c).wait_send()

    @pl.when(relays)
    def _():
        @pl.loop(0, chunks)
        def _(c):
            for d in range(2):
                @pl.loop(1, half)
                def _(k, d=d):
                    pass_on(d, k, c).wait_send()
                sum_out(d, c).wait_send()

    for i in range(3):
        @pl.loop(1, nb)
        def _(k, i=i):
            to_batch(i, k).wait_send()
        for j in range(nb):
            for k in range(1, nh):
                to_head(i, j, k).wait_send()


def body(hidden_in, norm_gain, w_gate, w_up, w_down, expert_ids, gate_codes, out_grad):
    n, nb, nh = (lax.axis_size(a) for a in ("expert", "batch", "head"))
    local, width, hidden = w_gate.shape
    experts = n * local
    tok, features = hidden_in.shape
    chosen = expert_ids.shape[1]
    cap = 3 * tok * chosen // (2 * experts)
    rows = -(-local * cap // 16) * 16
    chunks = nb * nh
    meta = jnp.concatenate([expert_ids, gate_codes], axis=1).T
    meta = jnp.pad(meta, ((0, -2 * chosen % 8), (0, 0)))
    numbers = np.arange(experts)
    base = (numbers // local * rows + numbers % local * cap).astype(np.float32)[:, None]
    pick = np.zeros((local, n * cap, n * rows), np.float32)
    for e in range(local):
        line = np.arange(n * cap)
        pick[e, line, line // cap * rows + e * cap + line % cap] = 1.0
    place = pick.transpose(0, 2, 1)
    flow = pltpu.VMEM((n * rows, features), BF)
    vmem = pl.BlockSpec(memory_space=pltpu.VMEM)
    hbm = pl.BlockSpec(memory_space=pl.ANY)
    dma = pltpu.SemaphoreType.DMA
    out_type = jax.ShapeDtypeStruct((tok, features), BF)
    return pl.pallas_call(
        functools.partial(kernel, (n, nb, nh, cap, rows, local, chosen)),
        out_shape=(out_type, out_type),
        in_specs=[vmem, vmem, hbm, hbm, hbm] + [vmem] * 5,
        out_specs=(vmem, vmem),
        scratch_shapes=[
            pltpu.VMEM((chunks, local, width, hidden), BF),
            pltpu.VMEM((chunks, local, width, hidden), BF),
            pltpu.VMEM((chunks, local, hidden, width), BF),
        ] + [flow] * 6 + [
            pltpu.VMEM((n // 2 * rows, features), BF),
            pltpu.VMEM((n // 2 * rows, features), BF),
            pltpu.VMEM((2, n // 2 * rows, features), BF),
            pltpu.VMEM((2, n // 2 * rows, features), BF),
            pltpu.VMEM((2, tok, features), BF),
            pltpu.VMEM((tok, features), BF),
            pltpu.VMEM((2, tok, features), BF),
            pltpu.VMEM((2,) + meta.shape, jnp.int32),
            pltpu.VMEM((2, 3, n // 2 * rows, tok), BF),
            pltpu.VMEM((local, n * cap, hidden), F32),
            pltpu.VMEM((local, n * cap, hidden), F32),
            pltpu.VMEM((tok, features), F32),
            pltpu.VMEM((3, n * rows, tok), BF),
            dma((3, n)), dma((3, n)), dma((2, n // 2, chunks)), dma((2, n // 2, chunks)),
            dma((n // 2, chunks)), dma((2, n // 2, chunks)), dma((3, chunks)), dma((2, chunks)), dma((chunks,)),
            dma((3,)),
            dma((3, nb)), dma((3, nb, nh)), dma((3, chunks)), dma((3,)),
        ],
        compiler_params=pltpu.CompilerParams(
            collective_id=0, has_side_effects=True, vmem_limit_bytes=60 * 1024 * 1024
        ),
    )(
        hidden_in, norm_gain[None], w_gate, w_up, w_down, meta, out_grad,
        jnp.asarray(base), jnp.asarray(pick, BF), jnp.asarray(place, BF),
    )


def solution(mesh):
    tokens = P(("batch", "head", "expert"), None)
    in_specs = (
        tokens,
        P(),
        P("expert", ("batch", "head"), None),
        P("expert", ("batch", "head"), None),
        P("expert", None, ("batch", "head")),
        tokens,
        tokens,
        tokens,
    )
    return jax.shard_map(body, mesh=mesh, in_specs=in_specs, out_specs=(tokens, tokens), check_vma=False)
```

```python
import functools

import jax
import jax.numpy as jnp
import numpy as np
from jax import lax
from jax.experimental import pallas as pl
from jax.experimental.pallas import tpu as pltpu
from jax.sharding import PartitionSpec as P

epsilon = 1e-06
MESH = pl.DeviceIdType.MESH
BF = jnp.bfloat16
F32 = jnp.float32
NN = (((1,), (0,)), ((), ()))
NT = (((1,), (1,)), ((), ()))
TN = (((0,), (0,)), ((), ()))


def mm(a, b, dims=NN):
    return lax.dot_general(a, b, dims, preferred_element_type=F32)


def kernel(
    sizes, hid, gain, wg_in, wu_in, wd_in, meta, og, base, pick, place, out, gin,
    wg, wu, wd, send_n, recv_n, recv_g, res, gres, ret, send_g, gret, pass_g, pass_r,
    far_og, far_part, far_sum, far_meta, far_table, gp, up, scaled, table,
    s_sem, r_sem, near_sem, pass_send, part_send, part_recv, og_sem, sum_send, sum_recv, meta_sem, wb_send, wh_send, w_recv, w_own,
):
    n, nb, nh, cap, rows, local, chosen = sizes
    me, mb, mh = (lax.axis_index(a) for a in ("expert", "batch", "head"))
    tok, features = hid.shape
    chunks = nb * nh
    width = features // chunks
    mine = mb * nh + mh
    peers = (("expert", me, n), ("batch", mb, nb), ("head", mh, nh))

    barrier = pltpu.get_barrier_semaphore()
    for axis, at, count in peers:
        @pl.loop(1, count)
        def _(k, axis=axis, at=at, count=count):
            pl.semaphore_signal(
                barrier, inc=1, device_id={axis: lax.rem(at + k, count)}, device_id_type=MESH
            )
    pl.semaphore_wait(barrier, n + nb + nh - 3)

    tensors = ((wg_in, wg), (wu_in, wu), (wd_in, wd))

    def to_batch(i, k):
        src, dst = tensors[i]
        other = lax.rem(mb + k, nb)
        return pltpu.make_async_remote_copy(
            src_ref=src, dst_ref=dst.at[mine], send_sem=wb_send.at[i, k], recv_sem=w_recv.at[i, mine],
            device_id={"batch": other}, device_id_type=MESH,
        )

    def to_head(i, j, k):
        src, dst = tensors[i]
        b = lax.rem(mb + j, nb)
        slot = b * nh + mh
        return pltpu.make_async_remote_copy(
            src_ref=src if j == 0 else dst.at[slot], dst_ref=dst.at[slot],
            send_sem=wh_send.at[i, j, k], recv_sem=w_recv.at[i, slot],
            device_id={"head": lax.rem(mh + k, nh)}, device_id_type=MESH,
        )

    def arrived(i, slot):
        dst = tensors[i][1].at[slot]
        pltpu.make_async_copy(dst, dst, w_recv.at[i, slot]).wait()

    def keep_own(i):
        return pltpu.make_async_copy(tensors[i][0], tensors[i][1].at[mine], w_own.at[i])

    quarter, half = n // 4, n // 2
    side, lane, q = me // half, lax.rem(me, quarter), me // quarter
    first = side * half
    relays = q == 1 + side
    turn = (1 - side) * (1 - q) + side * (q - 2)
    beyond = (2 - side) * quarter + lane

    def cols(c):
        return pl.ds(pl.multiple_of(c * width, 128), width)

    def source(d):
        return ((2 - side) + d * (1 - 2 * side)) * quarter + lane

    def remote(src, dst, send, recv, other):
        return pltpu.make_async_remote_copy(
            src_ref=src, dst_ref=dst, send_sem=send, recv_sem=recv,
            device_id={"expert": other}, device_id_type=MESH,
        )

    def meta_out():
        return remote(meta, far_meta.at[turn], meta_sem.at[0], meta_sem.at[1 + turn], beyond)

    def og_out(c):
        return remote(
            og.at[:, cols(c)], far_og.at[turn, :, cols(c)], og_sem.at[0, c], og_sem.at[1 + turn, c], beyond
        )

    def wait(ref, sem):
        pltpu.make_async_copy(ref, ref, sem).wait()

    early = chunks // 4
    meta_out().start()

    @pl.loop(0, early)
    def _(c):
        og_out(c).start()
    for i in range(3):
        @pl.loop(1, nb)
        def _(k, i=i):
            to_batch(i, k).start()
        keep_own(i).start()

    def block(ref, d):
        return ref.at[pl.ds(pl.multiple_of(d * rows, 16), rows)]

    def near(k):
        return first + lax.rem(me - first + k, half)

    def direct(step, k, c=None):
        other = near(k)
        if step == 1:
            src, dst = block(send_g, other - first), block(recv_g, me)
        else:
            other = lax.rem(me + 1 + lax.rem(k + half - 2, n - 1), n)
            src, dst = ((send_n, recv_n), None, (res, ret))[step]
            src, dst = block(src, other), block(dst, me)
        if c is not None:
            src, dst = src.at[:, cols(c)], dst.at[:, cols(c)]
        return remote(src, dst, s_sem.at[step, other], r_sem.at[step, me], other)

    homes = ((send_n, recv_n), (send_g, recv_g), (res, ret))
    spans = (n, half, n)

    def stream(step, c):
        @pl.loop(1, spans[step])
        def _(k):
            direct(step, k, c).start()

    def keep(step):
        src, dst = homes[step]
        at = me - first if step == 1 else me
        pltpu.make_async_copy(block(src, at), block(dst, me), r_sem.at[step, me]).start()

    def finish(step):
        dst = homes[step][1]

        @pl.loop(0, n)
        def _(j):
            wait(block(dst, j), r_sem.at[step, j])

    def piece(ref, j, c):
        return ref.at[pl.ds(pl.multiple_of(j * rows, 16), rows), cols(c)]

    def near_out(k, c):
        other = near(k)
        return remote(
            piece(gres, other, c), piece(gret, me - first, c),
            near_sem.at[0, k, c], near_sem.at[1, me - first, c], other,
        )

    def pass_on(d, k, c):
        other = near(k)
        return remote(
            piece(pass_g.at[d], other - first, c), piece(recv_g, source(d), c),
            pass_send.at[d, k, c], r_sem.at[1, source(d)], other,
        )

    def to_relay(k, c):
        s = half - first + k
        qs = s // quarter
        d = side * (1 - qs) + (1 - side) * (qs - 2)
        other = (1 + side) * quarter + lax.rem(s, quarter)
        src, dst = piece(gres, s, c), piece(pass_r.at[d], me - first, c)
        return other, src, dst, part_send.at[k, c], part_recv.at[d, me - first, c]

    def sum_out(d, c):
        return remote(
            far_sum.at[d, :, cols(c)], far_part.at[:, cols(c)], sum_send.at[d, c], sum_recv.at[c], source(d)
        )

    experts = base.shape[0]
    lower = (
        lax.broadcasted_iota(jnp.int32, (tok, tok), 0) < lax.broadcasted_iota(jnp.int32, (tok, tok), 1)
    ).astype(F32).astype(BF)

    def routing(words, begin, count):
        labels = lax.broadcasted_iota(jnp.int32, (experts, tok), 0)
        hits = [(words[k:k + 1] == labels).astype(F32) for k in range(chosen)]
        where = mm(functools.reduce(jnp.add, hits).astype(BF), lower) + base[...]
        slots = (lax.broadcasted_iota(jnp.int32, (count, tok), 0) + begin).astype(F32)
        marks = [(slots == jnp.sum(where * h, axis=0, keepdims=True)).astype(F32) for h in hits]
        code = [words[chosen + k:chosen + k + 1].astype(F32) for k in range(chosen)]
        total = functools.reduce(jnp.add, code)
        mix = functools.reduce(jnp.add, [m * (w / total) for m, w in zip(marks, code)])
        high = mix.astype(BF)
        low = (mix - high.astype(F32)).astype(BF)
        return functools.reduce(jnp.add, marks).astype(BF), high, low

    def combine(high, low, x):
        return mm(high, x, TN) + mm(low, x, TN)

    table[0], table[1], table[2] = routing(meta[...], 0, n * rows)
    own = pl.ds(pl.multiple_of(first * rows, 16), half * rows)

    def square(c, acc):
        v = hid[:, cols(c)].astype(F32)
        return acc + jnp.sum(v * v, axis=1, keepdims=True)

    zero = jnp.zeros((tok, 1), F32)
    scale = lax.rsqrt(lax.fori_loop(0, chunks, square, zero) / features + epsilon)

    @pl.loop(0, chunks)
    def _(c):
        v = (hid[:, cols(c)].astype(F32) * scale * gain[:, cols(c)]).astype(BF)
        send_n[:, cols(c)] = mm(table[0], v).astype(BF)
        stream(0, c)
    keep(0)

    @pl.loop(early, chunks)
    def _(c):
        og_out(c).start()

    @pl.loop(0, chunks)
    def _(c):
        send_g[:, cols(c)] = mm(table[0, own], og[:, cols(c)]).astype(BF)
        stream(1, c)
    keep(1)

    def forward_on(i):
        for j in range(nb):
            if j > 0:
                arrived(i, lax.rem(mb + j, nb) * nh + mh)
            for k in range(1, nh):
                to_head(i, j, k).start()

    def whole(i):
        keep_own(i).wait()
        for b in range(nb):
            for k in range(1, nh):
                arrived(i, b * nh + lax.rem(mh + k, nh))

    forward_on(0)
    forward_on(1)
    finish(0)
    whole(0)
    whole(1)
    gp[...] = jnp.zeros_like(gp)
    up[...] = jnp.zeros_like(up)

    @pl.loop(0, chunks)
    def _(c):
        x = recv_n[:, cols(c)]
        for e in range(local):
            xe = mm(pick[e], x).astype(BF)
            gp[e] += mm(xe, wg[c, e])
            up[e] += mm(xe, wu[c, e])

    @pl.when(relays)
    def _():
        for d in range(2):
            wait(far_meta.at[d], meta_sem.at[1 + d])
            far_table[d, 0], far_table[d, 1], far_table[d, 2] = routing(far_meta[d], first * rows, half * rows)

    def relay_grads(begin, end):
        @pl.when(relays)
        def _():
            @pl.loop(begin, end)
            def _(c):
                for d in range(2):
                    wait(far_og.at[d, :, cols(c)], og_sem.at[1 + d, c])
                    pass_g[d, :, cols(c)] = mm(far_table[d, 0], far_og[d, :, cols(c)]).astype(BF)

                    @pl.loop(1, half)
                    def _(k, d=d):
                        pass_on(d, k, c).start()
                    pltpu.make_async_copy(
                        piece(pass_g.at[d], me - first, c), piece(recv_g, source(d), c), r_sem.at[1, source(d)]
                    ).start()

    relay_grads(0, chunks // 2)
    forward_on(2)
    relay_grads(chunks // 2, chunks)
    whole(2)
    inner = [(jax.nn.silu(gp[e]) * up[e]).astype(BF) for e in range(local)]

    @pl.loop(0, chunks)
    def _(c):
        parts = [mm(place[e], mm(inner[e], wd[c, e]).astype(BF)) for e in range(local)]
        res[:, cols(c)] = functools.reduce(jnp.add, parts).astype(BF)
        stream(2, c)
    keep(2)

    finish(1)

    def back(c, acc):
        y = recv_g[:, cols(c)]
        return tuple(
            acc[e] + mm(mm(pick[e], y).astype(BF), wd[c, e], NT) for e in range(local)
        )

    none = tuple(jnp.zeros(gp.shape[1:], F32) for _ in range(local))
    grads = lax.fori_loop(0, chunks, back, none)
    g_gate, g_up = [], []
    for e in range(local):
        g = gp[e]
        s = jax.nn.sigmoid(g)
        g_gate.append((grads[e] * up[e] * s * (1.0 + g * (1.0 - s))).astype(BF))
        g_up.append((grads[e] * (g * s)).astype(BF))

    @pl.loop(0, chunks)
    def _(c):
        parts = []
        for e in range(local):
            r = mm(g_gate[e], wg[c, e], NT) + mm(g_up[e], wu[c, e], NT)
            parts.append(mm(place[e], r.astype(BF)))
        gres[:, cols(c)] = functools.reduce(jnp.add, parts).astype(BF)

        @pl.loop(0, half)
        def _(k):
            other, src, dst, send, recv = to_relay(k, c)

            @pl.when(other != me)
            def _():
                remote(src, dst, send, recv, other).start()

            @pl.when(other == me)
            def _():
                pltpu.make_async_copy(src, dst, recv).start()

    @pl.loop(0, chunks)
    def _(c):
        @pl.loop(1, half)
        def _(k):
            near_out(k, c).start()
        pltpu.make_async_copy(
            piece(gres, me, c), piece(gret, me - first, c), near_sem.at[1, me - first, c]
        ).start()

    def relay_sums(begin, end):
        @pl.when(relays)
        def _():
            @pl.loop(begin, end)
            def _(c):
                for d in range(2):
                    @pl.loop(0, half)
                    def _(j, d=d):
                        wait(piece(pass_r.at[d], j, c), part_recv.at[d, j, c])
                    x = pass_r[d, :, cols(c)]
                    far_sum[d, :, cols(c)] = combine(far_table[d, 1], far_table[d, 2], x).astype(BF)
                    sum_out(d, c).start()

    relay_sums(0, chunks // 2)
    finish(2)

    @pl.loop(0, chunks)
    def _(c):
        mixture = combine(table[1], table[2], ret[:, cols(c)])
        out[:, cols(c)] = (hid[:, cols(c)].astype(F32) + mixture).astype(BF)

    relay_sums(chunks // 2, chunks)

    def scaling(c, acc):
        @pl.loop(0, half)
        def _(j):
            wait(piece(gret, j, c), near_sem.at[1, j, c])
        wait(far_part.at[:, cols(c)], sum_recv.at[c])
        total = combine(table[1, own], table[2, own], gret[:, cols(c)]) + far_part[:, cols(c)].astype(F32)
        a = gain[:, cols(c)] * total
        scaled[:, cols(c)] = a
        return acc + jnp.sum(a * hid[:, cols(c)].astype(F32), axis=1, keepdims=True)

    mean = lax.fori_loop(0, chunks, scaling, zero) / features
    cubed = scale * scale * scale * mean

    @pl.loop(0, chunks)
    def _(c):
        gin[:, cols(c)] = (
            og[:, cols(c)].astype(F32) + scale * scaled[:, cols(c)] - hid[:, cols(c)].astype(F32) * cubed
        ).astype(BF)

    for step in range(3):
        @pl.loop(1, spans[step])
        def _(k, step=step):
            direct(step, k).wait_send()

    @pl.loop(0, chunks)
    def _(c):
        @pl.loop(0, half)
        def _(k):
            other, src, dst, send, recv = to_relay(k, c)

            @pl.when(other != me)
            def _():
                remote(src, dst, send, recv, other).wait_send()

        @pl.loop(1, half)
        def _(k):
            near_out(k, c).wait_send()
    meta_out().wait_send()

    @pl.loop(0, chunks)
    def _(c):
        og_out(c).wait_send()

    @pl.when(relays)
    def _():
        @pl.loop(0, chunks)
        def _(c):
            for d in range(2):
                @pl.loop(1, half)
                def _(k, d=d):
                    pass_on(d, k, c).wait_send()
                sum_out(d, c).wait_send()

    for i in range(3):
        @pl.loop(1, nb)
        def _(k, i=i):
            to_batch(i, k).wait_send()
        for j in range(nb):
            for k in range(1, nh):
                to_head(i, j, k).wait_send()


def body(hidden_in, norm_gain, w_gate, w_up, w_down, expert_ids, gate_codes, out_grad):
    n, nb, nh = (lax.axis_size(a) for a in ("expert", "batch", "head"))
    local, width, hidden = w_gate.shape
    experts = n * local
    tok, features = hidden_in.shape
    chosen = expert_ids.shape[1]
    cap = 3 * tok * chosen // (2 * experts)
    rows = -(-local * cap // 16) * 16
    chunks = nb * nh
    meta = jnp.concatenate([expert_ids, gate_codes], axis=1).T
    meta = jnp.pad(meta, ((0, -2 * chosen % 8), (0, 0)))
    numbers = np.arange(experts)
    base = (numbers // local * rows + numbers % local * cap).astype(np.float32)[:, None]
    pick = np.zeros((local, n * cap, n * rows), np.float32)
    for e in range(local):
        line = np.arange(n * cap)
        pick[e, line, line // cap * rows + e * cap + line % cap] = 1.0
    place = pick.transpose(0, 2, 1)
    flow = pltpu.VMEM((n * rows, features), BF)
    vmem = pl.BlockSpec(memory_space=pltpu.VMEM)
    hbm = pl.BlockSpec(memory_space=pl.ANY)
    dma = pltpu.SemaphoreType.DMA
    out_type = jax.ShapeDtypeStruct((tok, features), BF)
    return pl.pallas_call(
        functools.partial(kernel, (n, nb, nh, cap, rows, local, chosen)),
        out_shape=(out_type, out_type),
        in_specs=[vmem, vmem, hbm, hbm, hbm] + [vmem] * 5,
        out_specs=(vmem, vmem),
        scratch_shapes=[
            pltpu.VMEM((chunks, local, width, hidden), BF),
            pltpu.VMEM((chunks, local, width, hidden), BF),
            pltpu.VMEM((chunks, local, hidden, width), BF),
        ] + [flow] * 6 + [
            pltpu.VMEM((n // 2 * rows, features), BF),
            pltpu.VMEM((n // 2 * rows, features), BF),
            pltpu.VMEM((2, n // 2 * rows, features), BF),
            pltpu.VMEM((2, n // 2 * rows, features), BF),
            pltpu.VMEM((2, tok, features), BF),
            pltpu.VMEM((tok, features), BF),
            pltpu.VMEM((2, tok, features), BF),
            pltpu.VMEM((2,) + meta.shape, jnp.int32),
            pltpu.VMEM((2, 3, n // 2 * rows, tok), BF),
            pltpu.VMEM((local, n * cap, hidden), F32),
            pltpu.VMEM((local, n * cap, hidden), F32),
            pltpu.VMEM((tok, features), F32),
            pltpu.VMEM((3, n * rows, tok), BF),
            dma((3, n)), dma((3, n)), dma((2, n // 2, chunks)), dma((2, n // 2, chunks)),
            dma((n // 2, chunks)), dma((2, n // 2, chunks)), dma((3, chunks)), dma((2, chunks)), dma((chunks,)),
            dma((3,)),
            dma((3, nb)), dma((3, nb, nh)), dma((3, chunks)), dma((3,)),
        ],
        compiler_params=pltpu.CompilerParams(
            collective_id=0, has_side_effects=True, vmem_limit_bytes=60 * 1024 * 1024
        ),
    )(
        hidden_in, norm_gain[None], w_gate, w_up, w_down, meta, out_grad,
        jnp.asarray(base), jnp.asarray(pick, BF), jnp.asarray(place, BF),
    )


def solution(mesh):
    tokens = P(("batch", "head", "expert"), None)
    in_specs = (
        tokens,
        P(),
        P("expert", ("batch", "head"), None),
        P("expert", ("batch", "head"), None),
        P("expert", None, ("batch", "head")),
        tokens,
        tokens,
        tokens,
    )
    return jax.shard_map(body, mesh=mesh, in_specs=in_specs, out_specs=(tokens, tokens), check_vma=False)
```
